128 devices in a mesh: slab: 16 (over y, z), half: 2 (over core), img: 4 (over x).
Axes of the slice: x: 4, y: 4, z: 4, core: 2. Of those that a mesh axis runs over, the one named last changes fastest.
Arguments:
- samples: bfloat16 [8192, 2, 96, 128], P(('half', 'slab', 'img')), parts along dimension 0, may hold values from -6 to 6
- kernels: bfloat16 [64, 128, 128], replicated, may hold values from -0.5 to 0.5
- dest: int32 [8192, 1], P(('half', 'slab', 'img')), parts along dimension 0, may hold values from 0 to 15; in each aligned block of 64 rows (0 to 63, 64 to 127, ...) at most 8 rows name the same one
- plane_off: int32 [8192], P(('half', 'slab', 'img')), parts along dimension 0, may hold values from 0 to 31
- kernel_id: int32 [8192], P(('half', 'slab', 'img')), parts along dimension 0, may hold values from 0 to 63
Outputs:
- volume: float32 [2, 192, 512, 512], P(None, ('half', 'img'), 'slab'), parts along dimension 1
The draws below stay inside these ranges and needn't reach their ends.
There are 2 independent parts, one for each index of `half`. The reference program is written for one: setup_inputs(seed, part) draws one part's arguments, and reference() takes and returns one part's arrays. A program takes and returns all parts, laid end to end along the dimension named above; an argument that names none is the same for every part. Nothing has to cross between parts.
Inputs may be any that keep to these rules, and one draw needn't show every extreme that they name: `dest`: in each aligned block of 64 rows (the slice blocks of one device) no slab is named by more than 8 rows.
All inputs are finite; a program needn't handle non-finite values.
Results may differ from the reference program's by a relative error of at most 0.0003.
Values may be sent and summed in bfloat16 or wider, within the bound.
No kernel may reach another device: no remote copies, remote signals or barrier semaphores. Data moves between devices by JAX's collectives and lax.ppermute only.
A program may use at most 128 MiB of HBM per device.

```python
import math
import jax
import jax.numpy as jnp
import numpy as np
from jax import lax

NY = 512
NZ = 512
KW = 128
NK = 64
XW = 96
NB = 4
ITEMS_DEV = 64
ITEMS = 4096
ZL = 32
CAP = 8
N_SLAB = 16


def plant(values, key, low, top_value):
    place = [jax.random.randint(jax.random.fold_in(key, axis), (), 0, length) for axis, length in enumerate(values.shape)]
    longest = values.shape.index(max(values.shape))
    neighbour = place[:longest] + [(place[longest] + 1) % values.shape[longest]] + place[longest + 1:]
    return values.at[tuple(place)].set(low).at[tuple(neighbour)].set(top_value)


def block_scale(stream_key, extent, cuts, smallest, largest):
    factor_of, own = 1.0, jax.random.fold_in(stream_key, 6)
    for position, blocks in cuts:
        draws = jnp.exp(jax.random.uniform(jax.random.fold_in(own, position), (blocks,), jnp.float32, smallest / len(cuts), largest / len(cuts)))
        factor_of = factor_of * jnp.repeat(draws, extent[position] // blocks).reshape([-1 if axis == position else 1 for axis in range(len(extent))])
    return factor_of


def shared_out(own_key, own, number, rows, number_of, top, most, slope):
    order = jax.random.permutation(own_key, number_of)
    crowded, ordinary = portions_of(number_of, rows * top, most, slope, True), portions_of(number_of, rows * top, most, slope, False)
    places = jnp.arange(number_of)

    def named(lengths, offset_by):
        used = int((lengths > 0).sum())
        fixed = max(1, used // 4)
        passed = fixed + (places - fixed + offset_by * (used - fixed)) % max(1, number_of - fixed)
        return jnp.zeros((number_of,), jnp.int32).at[order[jnp.where(places < fixed, places, passed)]].set(jnp.asarray(lengths, jnp.int32))

    lengths = jnp.where(number % 4 == 0, named(crowded, number // 4), named(ordinary, number - number // 4 - 1))
    mixed = jax.random.permutation(jax.random.fold_in(own, 3), number_of)
    source_of, sink = mixed[0:number_of // 2 * 2:2], mixed[1:number_of // 2 * 2:2]
    slack = jnp.minimum(lengths[source_of] - 1, most - lengths[sink]) // 2
    slack = jnp.where((source_of == order[0]) | (sink == order[0]) | (lengths[sink] == 0), 0, jnp.maximum(slack, 0))
    passed = jax.random.randint(jax.random.fold_in(own, 4), (number_of // 2,), 0, 1 << 20) % (slack + 1)
    lengths = lengths.at[source_of].add(-passed).at[sink].add(passed)
    items = jnp.searchsorted(jnp.cumsum(lengths), jnp.arange(rows * top), side="right").astype(jnp.int32)
    table = items.reshape(top, rows).T
    table = table[jax.random.permutation(jax.random.fold_in(own, 1), rows)]
    offset_by = jax.random.randint(jax.random.fold_in(own, 2), (rows, 1), 0, top)
    return jnp.take_along_axis(table, (jnp.arange(top)[None, :] + offset_by) % top, axis=1)


def portions_of(count, total, most, skew, full):
    loads = [(1 << 20) // math.isqrt(grade ** skew) + 1 for grade in range(1, count + 1)]
    largest = most if full else min(most, max(-(-total // count), total * loads[0] // sum(loads)))
    least = 1 if total - largest >= count - 1 else 0
    given, rest = [largest] + [least] * (count - 1), total - largest - least * (count - 1)
    while rest > 0:
        free = [i for i in range(1, count) if given[i] < largest] or [i for i in range(1, count) if given[i] < most]
        pool, budget = sum([loads[i] for i in free]), rest
        for i in free:
            more = min(most - given[i], max(1, budget * loads[i] // pool), rest)
            given[i] = given[i] + more
            rest = rest - more
    return np.array(given)


def gaussian(stream_key, dims, width, most, split=(), held_as=jnp.bfloat16):
    array = jax.random.normal(stream_key, dims, jnp.float32) * width
    if len(split) > 0:
        array = block_scale(stream_key, dims, split, -0.22, 0.18) * array
    return jnp.clip(array, min=-most, max=most).astype(held_as)


def setup_inputs(seed: int = 0, part: int = 0) -> dict:
    seeds = jax.random.split(jax.random.key(seed), 6)
    part_keys = jax.random.split(jax.random.fold_in(seeds[5], part), 6)
    samples = gaussian(part_keys[0], (ITEMS, 2, XW, KW), 1.0, 6.0, ((0, 64),))
    kernels = gaussian(seeds[1], (NK, KW, KW), KW ** -0.5, 0.5)
    dest_keys = jax.random.split(jax.random.fold_in(part_keys[2], 1), ITEMS // ITEMS_DEV)
    dest_turns = jax.random.permutation(jax.random.fold_in(part_keys[2], 3), ITEMS // ITEMS_DEV)
    dest = jax.vmap(lambda own, number: shared_out(jax.random.fold_in(part_keys[2], 2), own, number, ITEMS_DEV, N_SLAB, 1, CAP, 2))(dest_keys, dest_turns).reshape((ITEMS, 1))
    plane_off = plant(jax.random.randint(part_keys[3], (ITEMS,), 0, ZL), jax.random.fold_in(part_keys[3], 1), 0, ZL - 1).astype(jnp.int32)
    kernel_id = plant(jax.random.randint(part_keys[4], (ITEMS,), 0, NK), jax.random.fold_in(part_keys[4], 1), 0, NK - 1).astype(jnp.int32)
    return {"samples": samples, "kernels": kernels, "dest": dest, "plane_off": plane_off, "kernel_id": kernel_id}


def reverse_bits(values):
    levels = N_SLAB.bit_length() - 1
    total = values * 0
    for level in range(levels):
        total = total + values // 2 ** level % 2 * 2 ** (levels - 1 - level)
    return total

def reference(samples, kernels, dest, plane_off, kernel_id):
    groups = ITEMS // ITEMS_DEV
    planes = (N_SLAB * plane_off + reverse_bits(dest[:, 0])).astype(jnp.int32)
    blocks = (jnp.arange(ITEMS, dtype=jnp.int32) % NB).astype(jnp.int32)

    def add_group(grid, pieces):
        sample_rows, kernel_rows, plane_rows, block_rows = pieces
        tables = kernels[kernel_rows].astype(jnp.float32)
        contrib = jnp.einsum('mrxk,mkj->mxrj', sample_rows.astype(jnp.float32), tables, precision=lax.Precision.HIGHEST)
        grid = grid.at[:, plane_rows, :, block_rows, :].add(contrib)
        return (grid, None)
    start_grid = jnp.zeros((XW, NZ, 2, NB, KW), jnp.float32)
    pieces = (samples.reshape(groups, ITEMS_DEV, 2, XW, KW), kernel_id.reshape(groups, ITEMS_DEV), planes.reshape(groups, ITEMS_DEV), blocks.reshape(groups, ITEMS_DEV))
    grid, unused = lax.scan(add_group, start_grid, pieces)
    grid = grid.reshape(XW, NZ, 2, NY)
    complex_grid = grid[:, :, 0, :] + 1j * grid[:, :, 1, :]
    result = jnp.fft.ifft2(complex_grid, axes=(1, 2)) * math.sqrt(NY * NZ)
    return jnp.stack([jnp.real(result), jnp.imag(result)], axis=0).astype(jnp.float32)
```

```python
import functools
import math

import jax
import jax.numpy as jnp
import ml_dtypes
import numpy as np
from jax import lax
from jax.experimental import pallas as pl
from jax.experimental.pallas import tpu as pltpu
from jax.sharding import PartitionSpec as P

NY = 512
NZ = 512
KW = 128
N_SLAB = 16
N_IMG = 4
N_DEST = N_SLAB * N_IMG
ITEMS = 64
XW = 96
X_OWN = XW // N_IMG
X3 = 3
ROWS = 2 * XW
Q = 2 * X3
A_ROWS = Q * 32 + 8
B_ROWS = 2 * Q * 32 + 8
LEVEL = 32700.0
TINY = 1e-30
STEP_ITEMS = 8
T_BLOCK = 2
VMEM_LIMIT = 60 * 1024 * 1024


def split_bf16(values):
    high = values.astype(ml_dtypes.bfloat16)
    low = (values - high.astype(np.float64)).astype(ml_dtypes.bfloat16)
    return high, low


def complex_table(factor):
    return np.block([[factor.real, factor.imag], [-factor.imag, factor.real]])


@functools.lru_cache(None)
def constants():
    j_even = 2 * np.arange(64)
    perm = np.zeros((KW, 2 * KW))
    for b1, order in enumerate(
        (np.concatenate([j_even, j_even + 1]), np.concatenate([j_even + 1, j_even]))
    ):
        perm[order, b1 * KW + np.arange(KW)] = 1.0
    z_tables = []
    for rho in range(4):
        z = 4 * np.arange(128) + rho
        k = np.arange(128)
        factor = np.exp(2j * np.pi * (np.outer(k, z) % NZ) / NZ)
        z_tables.append(
            np.block([[factor.real, -factor.imag], [factor.imag, factor.real]])
        )
    y_tables = []
    for parity in range(2):
        blocks = (0, 1) if parity == 0 else (1, 0)
        y = np.concatenate(
            [(2 * p + b1) * KW + j_even + parity for p in range(2) for b1 in blocks]
        )
        v = np.arange(256)
        factor = np.exp(2j * np.pi * (np.outer(y, v) % NY) / NY) / math.sqrt(NY * NZ)
        y_tables.append(complex_table(factor))
    return (
        perm.astype(ml_dtypes.bfloat16),
        split_bf16(np.stack(z_tables)),
        split_bf16(np.stack(y_tables)),
    )


def dot(a, b):
    return jnp.dot(a, b, preferred_element_type=jnp.float32)


def halves(value):
    high = value.astype(jnp.bfloat16)
    return high, (value - high.astype(jnp.float32)).astype(jnp.bfloat16)


def scale_codes(largest):
    return jnp.ceil(jnp.log2(jnp.maximum(largest, TINY)) * 256.0)


def to_codes(value, inverse):
    return jnp.round(value * inverse).astype(jnp.int32).astype(jnp.int16)


def from_codes(codes):
    return codes.astype(jnp.int32).astype(jnp.float32)


def scales_of(tail):
    return jnp.exp2(tail * (1.0 / 256.0)) * (1.0 / LEVEL)


def spread_kernel(
    dest_s, plane_s, kid_s, samples_ref, kernels_ref, perm_ref, out_ref, table_ref, rows_ref, label_ref
):
    step = pl.program_id(0)
    lane = lax.broadcasted_iota(jnp.int32, (1, KW), 1)

    @pl.when(step == 0)
    def _():
        table = kernels_ref[...].reshape(64 * KW, KW)
        table_ref[...] = dot(table, perm_ref[...]).astype(jnp.bfloat16)
        label_ref[...] = jnp.zeros_like(label_ref)

    for u in range(STEP_ITEMS):
        item = step * STEP_ITEMS + u
        block = u % 4
        pair, b1 = block // 2, block % 2
        g = step * (STEP_ITEMS // 4) + u // 4
        kid = kid_s[item]
        table = table_ref[pl.ds(pl.multiple_of(kid * KW, KW), KW), b1 * KW : (b1 + 1) * KW]
        value = dot(samples_ref[u].reshape(ROWS, KW), table)
        rows_ref[pl.ds(pair * ROWS * 32 + b1 * 16 + g, ROWS, stride=32), :] = value
        d = dest_s[item]
        flipped = ((d & 1) << 3) | ((d & 2) << 1) | ((d & 4) >> 1) | ((d & 8) >> 3)
        plane = plane_s[item] * 16 + flipped
        place = (plane & 3) * 128 + (plane >> 2)
        row = 8 * pair + 6 + b1
        label_ref[row : row + 1, :] = jnp.where(
            (lane & 15) == g, place, label_ref[row : row + 1, :]
        )

    @pl.when(step == pl.num_programs(0) - 1)
    def _():
        def one(d, carry):
            pair = d // 32
            first = X_OWN * (d % 4) + X3 * ((d // 4) % 8)
            values, tops = [], []
            for r in range(2):
                for x3 in range(X3):
                    start = (pair * ROWS + r * XW + first + x3) * 32
                    value = rows_ref[pl.ds(pl.multiple_of(start, 32), 32), :]
                    values.append(value)
                    tops.append(jnp.max(jnp.abs(value), axis=0, keepdims=True))
            tops = jnp.concatenate(tops + [tops[0], tops[0]], axis=0)
            codes = scale_codes(tops)
            inverse = jnp.exp2(codes * (-1.0 / 256.0)) * LEVEL
            for q in range(Q):
                out_ref[d, q * 32 : (q + 1) * 32, :] = to_codes(values[q], inverse[q : q + 1])
            labels = label_ref[pl.ds(pl.multiple_of(pair * 8, 8), 8), :]
            sub = lax.broadcasted_iota(jnp.int32, (8, KW), 0)
            tail = jnp.where(sub < Q, codes.astype(jnp.int32), labels)
            out_ref[d, Q * 32 : A_ROWS, :] = tail.astype(jnp.int16)
            return carry

        lax.fori_loop(0, N_DEST, one, 0)


def plane_kernel(
    got_ref, wh_ref, wl_ref, out_ref, hot_ref, xh_ref, xl_ref, grid_ref, freq_ref
):
    lane = lax.broadcasted_iota(jnp.int32, (1, KW), 1)
    place = lax.broadcasted_iota(jnp.int32, (NZ, KW), 0)

    def unpack(src, carry):
        tail = from_codes(got_ref[src, Q * 32 : A_ROWS, :])
        scale = scales_of(tail)
        at = pl.ds(pl.multiple_of(src * 16, 16), 16)
        for b1 in range(2):
            for q in range(Q):
                codes = got_ref[src, q * 32 + b1 * 16 : q * 32 + b1 * 16 + 16, :]
                high, low = halves(from_codes(codes) * scale[q : q + 1])
                xh_ref[b1, at, q * KW : (q + 1) * KW] = high
                xl_ref[b1, at, q * KW : (q + 1) * KW] = low
        return carry

    lax.fori_loop(0, N_DEST, unpack, 0)
    for group in range(8):
        rows = [jnp.zeros((1, KW), jnp.int32), jnp.zeros((1, KW), jnp.int32)]
        for e in range(8):
            tail = got_ref[group * 8 + e, Q * 32 : A_ROWS, :].astype(jnp.int32)
            for b1 in range(2):
                rows[b1] = jnp.where((lane >> 4) == e, tail[6 + b1 : 7 + b1], rows[b1])
        for b1 in range(2):
            hit = jnp.where(place == rows[b1], 1.0, 0.0).astype(jnp.bfloat16)
            hot_ref[b1, :, group * KW : (group + 1) * KW] = hit
    for b1 in range(2):
        grid_ref[b1] = dot(hot_ref[b1], xh_ref[b1]) + dot(hot_ref[b1], xl_ref[b1])
    side = (lax.broadcasted_iota(jnp.int32, (1, X3 * KW), 1) & 64) == 0
    for rho in range(4):
        parts = []
        for r in range(2):
            at = (slice(rho * 128, (rho + 1) * 128), slice(r * X3 * KW, (r + 1) * X3 * KW))
            even, odd = grid_ref[0, at[0], at[1]], grid_ref[1, at[0], at[1]]
            parts.append(
                jnp.concatenate([jnp.where(side, even, odd), jnp.where(side, odd, even)], axis=1)
            )
        high, low = halves(jnp.concatenate(parts, axis=0))
        freq_ref[rho] = dot(wh_ref[rho], high) + dot(wh_ref[rho], low) + dot(wl_ref[rho], high)

    def send(kk, carry):
        for tile in range(2 * X3):
            cols = slice(tile * KW, (tile + 1) * KW)
            re = [freq_ref[rho, pl.ds(pl.multiple_of(kk * 32, 32), 32), cols] for rho in range(4)]
            im = [
                freq_ref[rho, pl.ds(pl.multiple_of(kk * 32 + 128, 32), 32), cols]
                for rho in range(4)
            ]
            sr, dr, tr, er = re[0] + re[2], re[0] - re[2], re[1] + re[3], re[1] - re[3]
            si, di, ti, ei = im[0] + im[2], im[0] - im[2], im[1] + im[3], im[1] - im[3]
            out = ((sr + tr, si + ti), (dr - ei, di + er), (sr - tr, si - ti), (dr + ei, di - er))
            for a in range(4):
                value_re, value_im = out[a]
                top = jnp.max(
                    jnp.maximum(jnp.abs(value_re), jnp.abs(value_im)), axis=0, keepdims=True
                )
                codes = scale_codes(top)
                inverse = jnp.exp2(codes * (-1.0 / 256.0)) * LEVEL
                base = tile * 64
                out_ref[4 * a + kk, base : base + 32, :] = to_codes(value_re, inverse)
                out_ref[4 * a + kk, base + 32 : base + 64, :] = to_codes(value_im, inverse)
                tails[a].append(codes)
        return carry

    tails = [[], [], [], []]
    for kk in range(4):
        for a in range(4):
            tails[a].clear()
        send(kk, 0)
        for a in range(4):
            rows = jnp.concatenate(tails[a] + [tails[a][0], tails[a][0]], axis=0)
            out_ref[4 * a + kk, 2 * Q * 32 : B_ROWS, :] = rows.astype(jnp.int32).astype(jnp.int16)


def line_kernel(got_ref, wh_ref, wl_ref, out_ref, xh_ref, xl_ref):
    for t in range(T_BLOCK):
        for p in range(2):
            scale = scales_of(from_codes(got_ref[p, t, 2 * Q * 32 : B_ROWS, :]))
            for parity in range(2):
                for x3 in range(X3):
                    tile = parity * X3 + x3
                    row = (t * X3 + x3) * 32
                    for c in range(2):
                        codes = got_ref[p, t, tile * 64 + c * 32 : tile * 64 + c * 32 + 32, :]
                        high, low = halves(from_codes(codes) * scale[tile : tile + 1])
                        col = (c * 2 + p) * KW
                        xh_ref[parity, row : row + 32, col : col + KW] = high
                        xl_ref[parity, row : row + 32, col : col + KW] = low
    sums = []
    for parity in range(2):
        high, low = xh_ref[parity], xl_ref[parity]
        sums.append(
            dot(high, wh_ref[parity]) + dot(low, wh_ref[parity]) + dot(high, wl_ref[parity])
        )
    near, far = sums[0] + sums[1], sums[0] - sums[1]
    for row in range(T_BLOCK * X3):
        at = slice(row * 32, (row + 1) * 32)
        for c in range(2):
            out_ref[c, row, :, 0:256] = near[at, c * 256 : (c + 1) * 256]
            out_ref[c, row, :, 256:512] = far[at, c * 256 : (c + 1) * 256]


def per_device(samples, kernels, dest, plane_off, kernel_id):
    perm, (zh, zl), (yh, yl) = constants()
    params = pltpu.CompilerParams(
        dimension_semantics=("arbitrary",), vmem_limit_bytes=VMEM_LIMIT
    )
    whole = pl.BlockSpec(memory_space=pltpu.VMEM)
    packed = pl.pallas_call(
        spread_kernel,
        name="spread",
        out_shape=jax.ShapeDtypeStruct((N_DEST, A_ROWS, KW), jnp.int16),
        grid_spec=pltpu.PrefetchScalarGridSpec(
            num_scalar_prefetch=3,
            grid=(ITEMS // STEP_ITEMS,),
            in_specs=[
                pl.BlockSpec((STEP_ITEMS, 2, XW, KW), lambda i, *_: (i, 0, 0, 0)),
                whole,
                whole,
            ],
            out_specs=pl.BlockSpec((N_DEST, A_ROWS, KW), lambda i, *_: (0, 0, 0)),
            scratch_shapes=[
                pltpu.VMEM((64 * KW, 2 * KW), jnp.bfloat16),
                pltpu.VMEM((2 * ROWS * 32, KW), jnp.float32),
                pltpu.VMEM((16, KW), jnp.int32),
            ],
        ),
        compiler_params=params,
    )(dest.reshape(ITEMS), plane_off, kernel_id, samples, kernels, jnp.asarray(perm))
    got = lax.all_to_all(packed, ("slab", "img"), split_axis=0, concat_axis=0, tiled=True)
    planes = pl.pallas_call(
        plane_kernel,
        name="plane",
        out_shape=jax.ShapeDtypeStruct((N_SLAB, B_ROWS, KW), jnp.int16),
        in_specs=[whole, whole, whole],
        out_specs=whole,
        scratch_shapes=[
            pltpu.VMEM((2, NZ, 1024), jnp.bfloat16),
            pltpu.VMEM((2, 1024, Q * KW), jnp.bfloat16),
            pltpu.VMEM((2, 1024, Q * KW), jnp.bfloat16),
            pltpu.VMEM((2, NZ, Q * KW), jnp.float32),
            pltpu.VMEM((4, 256, Q * KW), jnp.float32),
        ],
        compiler_params=pltpu.CompilerParams(vmem_limit_bytes=VMEM_LIMIT),
    )(got, jnp.asarray(zh), jnp.asarray(zl))
    lines = lax.all_to_all(planes, "slab", split_axis=0, concat_axis=0, tiled=True)
    lines = lines.reshape(2, N_SLAB // 2, B_ROWS, KW)
    rows = T_BLOCK * X3
    return pl.pallas_call(
        line_kernel,
        name="line",
        out_shape=jax.ShapeDtypeStruct((2, X_OWN, NZ // N_SLAB, NY), jnp.float32),
        grid=(8 // T_BLOCK,),
        in_specs=[
            pl.BlockSpec((2, T_BLOCK, B_ROWS, KW), lambda i: (0, i, 0, 0)),
            whole,
            whole,
        ],
        out_specs=pl.BlockSpec((2, rows, NZ // N_SLAB, NY), lambda i: (0, i, 0, 0)),
        scratch_shapes=[
            pltpu.VMEM((2, rows * 32, 512), jnp.bfloat16),
            pltpu.VMEM((2, rows * 32, 512), jnp.bfloat16),
        ],
        compiler_params=params,
    )(lines, jnp.asarray(yh), jnp.asarray(yl))


def solution(mesh):
    in_specs = (
        P(("half", "slab", "img"), None, None, None),
        P(),
        P(("half", "slab", "img"), None),
        P(("half", "slab", "img")),
        P(("half", "slab", "img")),
    )
    out_specs = P(None, ("half", "img"), "slab", None)
    return jax.shard_map(
        per_device, mesh=mesh, in_specs=in_specs, out_specs=out_specs, check_vma=False
    )
```

```python
import functools
import math

import jax
import jax.numpy as jnp
import ml_dtypes
import numpy as np
from jax import lax
from jax.experimental import pallas as pl
from jax.experimental.pallas import tpu as pltpu
from jax.sharding import PartitionSpec as P

NY = 512
NZ = 512
KW = 128
N_SLAB = 16
N_IMG = 4
N_DEST = N_SLAB * N_IMG
ITEMS = 64
XW = 96
X_OWN = XW // N_IMG
X3 = 3
ROWS = 2 * XW
Q = 2 * X3
A_ROWS = Q * 32 + 8
B_ROWS = 2 * Q * 32 + 8
PITCH = 33
LEVEL = 32700.0
TINY = 1e-30
STEP_ITEMS = 8
ITEM_STEPS = ITEMS // STEP_ITEMS
STEP_DESTS = 8
T_BLOCK = 2
VMEM_LIMIT = 60 * 1024 * 1024


def split_bf16(values):
    high = values.astype(ml_dtypes.bfloat16)
    low = (values - high.astype(np.float64)).astype(ml_dtypes.bfloat16)
    return high, low


def y_orders():
    lane = np.arange(KW)
    order = {}
    for pair in range(2):
        a, b, c, d = (0, 1, 2, 3) if pair == 0 else (1, 0, 3, 2)
        for b1, runs in enumerate(((a, c, b, d), (c, a, d, b))):
            order[pair, b1] = np.concatenate([4 * np.arange(32) + r for r in runs])
    y = {key: (2 * key[0] + key[1]) * KW + j for key, j in order.items()}
    near = (lane & 32) == 0
    first = [np.where(near, y[p, 0], y[p, 1]) for p in range(2)]
    second = [np.where(near, y[p, 1], y[p, 0]) for p in range(2)]
    low = lane < 64
    tiles = [
        np.where(low, first[0], first[1]),
        np.where(low, first[1], first[0]),
        np.where(low, second[0], second[1]),
        np.where(low, second[1], second[0]),
    ]
    for rho in range(4):
        assert np.all(tiles[rho] % 4 == rho)
    return order, tiles


@functools.lru_cache(None)
def constants():
    order, tiles = y_orders()
    perm = np.zeros((4, KW, KW))
    for (pair, b1), j in order.items():
        perm[2 * pair + b1, j, np.arange(KW)] = 1.0
    k = np.arange(128)
    z_tables, y_tables = [], []
    for rho in range(4):
        factor = np.exp(2j * np.pi * (np.outer(k, 4 * k + rho) % NZ) / NZ)
        high, low = split_bf16(
            np.block([[factor.real, -factor.imag], [factor.imag, factor.real]])
        )
        z_tables.append(np.concatenate([high, high, low], axis=1))
        factor = np.exp(2j * np.pi * (np.outer(tiles[rho], k) % NY) / NY) / math.sqrt(NY * NZ)
        high, low = split_bf16(
            np.block([[factor.real, factor.imag], [-factor.imag, factor.real]])
        )
        y_tables.append(np.concatenate([high, high, low], axis=0))
    return perm.astype(ml_dtypes.bfloat16), np.stack(z_tables), np.stack(y_tables)


def dot(a, b):
    return jnp.dot(a, b, preferred_element_type=jnp.float32)


def halves(value):
    high = value.astype(jnp.bfloat16)
    return high, (value - high.astype(jnp.float32)).astype(jnp.bfloat16)


def scale_codes(largest):
    return jnp.ceil(jnp.log2(jnp.maximum(largest, TINY)) * 256.0)


def to_codes(value, inverse):
    return jnp.round(value * inverse).astype(jnp.int32).astype(jnp.int16)


def from_codes(codes):
    return codes.astype(jnp.int32).astype(jnp.float32)


def scales_of(tail):
    return jnp.exp2(tail * (1.0 / 256.0)) * (1.0 / LEVEL)


def radix_4(re, im):
    sr, dr, tr, er = re[0] + re[2], re[0] - re[2], re[1] + re[3], re[1] - re[3]
    si, di, ti, ei = im[0] + im[2], im[0] - im[2], im[1] + im[3], im[1] - im[3]
    return (sr + tr, si + ti), (dr - ei, di + er), (sr - tr, si - ti), (dr + ei, di - er)


def spread_kernel(
    dest_s, plane_s, kid_s, samples_ref, kernels_ref, perm_ref, out_ref, rows_ref, label_ref
):
    step = pl.program_id(0)
    lane = lax.broadcasted_iota(jnp.int32, (1, KW), 1)

    @pl.when(step == 0)
    def _():
        label_ref[...] = jnp.zeros_like(label_ref)

    @pl.when(step < ITEM_STEPS)
    def _():
        tables = [None] * STEP_ITEMS
        for block in range(4):
            mine = range(block, STEP_ITEMS, 4)
            raw = [kernels_ref[kid_s[step * STEP_ITEMS + u]] for u in mine]
            ordered = dot(jnp.concatenate(raw, axis=0), perm_ref[block]).astype(jnp.bfloat16)
            for n, u in enumerate(mine):
                tables[u] = ordered[n * KW : (n + 1) * KW]
        for u in range(STEP_ITEMS):
            item = step * STEP_ITEMS + u
            block = u % 4
            pair, b1 = block // 2, block % 2
            g = step * (STEP_ITEMS // 4) + u // 4
            value = dot(samples_ref[u].reshape(ROWS, KW), tables[u])
            rows_ref[pl.ds(pair * ROWS * PITCH + b1 * 16 + g, ROWS, stride=PITCH), :] = value
            d = dest_s[item]
            flipped = ((d & 1) << 3) | ((d & 2) << 1) | ((d & 4) >> 1) | ((d & 8) >> 3)
            plane = plane_s[item] * 16 + flipped
            place = (plane & 3) * 128 + (plane >> 2)
            row = 8 * pair + 6 + b1
            label_ref[row : row + 1, :] = jnp.where(
                (lane & 15) == g, place, label_ref[row : row + 1, :]
            )

    @pl.when(step >= ITEM_STEPS)
    def _():
        sub = lax.broadcasted_iota(jnp.int32, (8, KW), 0)

        def one(n, carry):
            d = (step - ITEM_STEPS) * STEP_DESTS + n
            pair = (d % N_SLAB) // 8
            first = pair * ROWS + X_OWN * (d // N_SLAB) + X3 * (d % 8)
            values, tops = [], []
            for r in range(2):
                for x3 in range(X3):
                    value = rows_ref[pl.ds((first + r * XW + x3) * PITCH, 32), :]
                    values.append(value)
                    tops.append(jnp.max(jnp.abs(value), axis=0, keepdims=True))
            codes = scale_codes(jnp.concatenate(tops + [tops[0], tops[0]], axis=0))
            inverse = jnp.exp2(codes * (-1.0 / 256.0)) * LEVEL
            for q in range(Q):
                out_ref[n, q * 32 : (q + 1) * 32, :] = to_codes(values[q], inverse[q : q + 1])
            labels = label_ref[pl.ds(pl.multiple_of(pair * 8, 8), 8), :]
            tail = jnp.where(sub < Q, codes.astype(jnp.int32), labels)
            out_ref[n, Q * 32 : A_ROWS, :] = tail.astype(jnp.int16)
            return carry

        lax.fori_loop(0, STEP_DESTS, one, 0, unroll=2)


def plane_kernel(got_ref, w_ref, out_ref, hot_ref, xh_ref, xl_ref, freq_ref, scale_ref):
    lane = lax.broadcasted_iota(jnp.int32, (1, KW), 1)
    place = lax.broadcasted_iota(jnp.int32, (NZ, KW), 0)
    near = (lane & 32) == 0
    for group in range(8):
        rows = [jnp.zeros((1, KW), jnp.int32), jnp.zeros((1, KW), jnp.int32)]
        for e in range(8):
            src = group * 8 + e
            tail = got_ref[src, Q * 32 : A_ROWS, :].astype(jnp.int32)
            scale_ref[src] = scales_of(tail.astype(jnp.float32))
            for b1 in range(2):
                rows[b1] = jnp.where((lane >> 4) == e, tail[6 + b1 : 7 + b1], rows[b1])
        for b1 in range(2):
            hit = jnp.where(place == rows[b1], 1.0, 0.0).astype(jnp.bfloat16)
            hot_ref[b1, :, group * KW : (group + 1) * KW] = hit
    codes_of = [[[None] * 2 for _ in range(X3)] for _ in range(N_SLAB)]
    for x3 in range(X3):
        for src in range(N_DEST):
            for r in range(2):
                q = r * X3 + x3
                for b1 in range(2):
                    codes = got_ref[src, q * 32 + b1 * 16 : q * 32 + b1 * 16 + 16, :]
                    high, low = halves(from_codes(codes) * scale_ref[src, q : q + 1, :])
                    xh_ref[x3, b1, src * 16 : src * 16 + 16, r * KW : (r + 1) * KW] = high
                    xl_ref[x3, b1, src * 16 : src * 16 + 16, r * KW : (r + 1) * KW] = low
        grid = [
            dot(hot_ref[b1], xh_ref[x3, b1]) + dot(hot_ref[b1], xl_ref[x3, b1])
            for b1 in range(2)
        ]
        for rho in range(4):
            at = slice(rho * 128, (rho + 1) * 128)
            parts = []
            for r in range(2):
                cols = slice(r * KW, (r + 1) * KW)
                t0, t1 = grid[0][at, cols], grid[1][at, cols]
                parts.append(
                    jnp.concatenate([jnp.where(near, t0, t1), jnp.where(near, t1, t0)], axis=1)
                )
            high, low = halves(jnp.concatenate(parts, axis=0))
            freq_ref[x3, rho] = dot(w_ref[rho], jnp.concatenate([high, low, high], axis=0))
        for kk in range(4):
            tops = [[], [], [], []]
            for tile in range(2):
                cols = slice(tile * KW, (tile + 1) * KW)
                at_re, at_im = slice(kk * 32, kk * 32 + 32), slice(128 + kk * 32, 160 + kk * 32)
                out = radix_4(
                    [freq_ref[x3, rho, at_re, cols] for rho in range(4)],
                    [freq_ref[x3, rho, at_im, cols] for rho in range(4)],
                )
                for a in range(4):
                    freq_ref[x3, a, at_re, cols] = out[a][0]
                    freq_ref[x3, a, at_im, cols] = out[a][1]
                    top = jnp.maximum(jnp.abs(out[a][0]), jnp.abs(out[a][1]))
                    tops[a].append(jnp.max(top, axis=0, keepdims=True))
            codes = scale_codes(jnp.concatenate(tops[0] + tops[1] + tops[2] + tops[3], axis=0))
            inverse = jnp.exp2(codes * (-1.0 / 256.0)) * LEVEL
            for a in range(4):
                for tile in range(2):
                    cols = slice(tile * KW, (tile + 1) * KW)
                    n = 2 * a + tile
                    codes_of[4 * a + kk][x3][tile] = codes[n : n + 1]
                    base = (x3 * 2 + tile) * 64
                    for c in range(2):
                        value = freq_ref[x3, a, c * 128 + kk * 32 : c * 128 + kk * 32 + 32, cols]
                        out_ref[4 * a + kk, base + c * 32 : base + c * 32 + 32, :] = to_codes(
                            value, inverse[n : n + 1]
                        )
    for s in range(N_SLAB):
        rows = [codes_of[s][x3][tile] for x3 in range(X3) for tile in range(2)]
        rows = jnp.concatenate(rows + rows[:2], axis=0)
        out_ref[s, 2 * Q * 32 : B_ROWS, :] = rows.astype(jnp.int32).astype(jnp.int16)


def line_kernel(got_ref, w_ref, out_ref, x_ref):
    low_half = lax.broadcasted_iota(jnp.int32, (1, KW), 1) < 64
    for t in range(T_BLOCK):
        scale = [scales_of(from_codes(got_ref[p, t, 2 * Q * 32 : B_ROWS, :])) for p in range(2)]
        for x3 in range(X3):
            row = (t * X3 + x3) * 32
            for tile in range(2):
                n = x3 * 2 + tile
                for c in range(2):
                    base = n * 64 + c * 32
                    v0, v1 = (
                        from_codes(got_ref[p, t, base : base + 32, :]) * scale[p][n : n + 1]
                        for p in range(2)
                    )
                    for half in range(2):
                        value = jnp.where(low_half, v0, v1) if half == 0 else jnp.where(low_half, v1, v0)
                        high, low = halves(value)
                        rho = 2 * tile + half
                        for third, part in enumerate((high, low, high)):
                            col = third * 256 + c * KW
                            x_ref[rho, row : row + 32, col : col + KW] = part
    parts = [dot(x_ref[rho], w_ref[rho]) for rho in range(4)]
    for row in range(T_BLOCK * X3):
        at = slice(row * 32, (row + 1) * 32)
        out = radix_4([p[at, :KW] for p in parts], [p[at, KW:] for p in parts])
        for a in range(4):
            for c in range(2):
                out_ref[c, row, :, a * KW : (a + 1) * KW] = out[a][c]


def per_device(samples, kernels, dest, plane_off, kernel_id):
    perm, z_table, y_table = constants()
    params = pltpu.CompilerParams(
        dimension_semantics=("arbitrary",), vmem_limit_bytes=VMEM_LIMIT
    )
    whole = pl.BlockSpec(memory_space=pltpu.VMEM)
    packed = pl.pallas_call(
        spread_kernel,
        name="spread",
        out_shape=jax.ShapeDtypeStruct((N_DEST, A_ROWS, KW), jnp.int16),
        grid_spec=pltpu.PrefetchScalarGridSpec(
            num_scalar_prefetch=3,
            grid=(ITEM_STEPS + N_DEST // STEP_DESTS,),
            in_specs=[
                pl.BlockSpec(
                    (STEP_ITEMS, 2, XW, KW),
                    lambda i, *_: (jnp.minimum(i, ITEM_STEPS - 1), 0, 0, 0),
                ),
                whole,
                whole,
            ],
            out_specs=pl.BlockSpec(
                (STEP_DESTS, A_ROWS, KW), lambda i, *_: (jnp.maximum(i - ITEM_STEPS, 0), 0, 0)
            ),
            scratch_shapes=[
                pltpu.VMEM((2 * ROWS * PITCH, KW), jnp.float32),
                pltpu.VMEM((16, KW), jnp.int32),
            ],
        ),
        compiler_params=params,
    )(dest.reshape(ITEMS), plane_off, kernel_id, samples, kernels, jnp.asarray(perm))
    got = lax.all_to_all(packed, ("img", "slab"), split_axis=0, concat_axis=0, tiled=True)
    planes = pl.pallas_call(
        plane_kernel,
        name="plane",
        out_shape=jax.ShapeDtypeStruct((N_SLAB, B_ROWS, KW), jnp.int16),
        in_specs=[whole, whole],
        out_specs=whole,
        scratch_shapes=[
            pltpu.VMEM((2, NZ, 1024), jnp.bfloat16),
            pltpu.VMEM((X3, 2, 1024, 256), jnp.bfloat16),
            pltpu.VMEM((X3, 2, 1024, 256), jnp.bfloat16),
            pltpu.VMEM((X3, 4, 256, 256), jnp.float32),
            pltpu.VMEM((N_DEST, 8, KW), jnp.float32),
        ],
        compiler_params=pltpu.CompilerParams(vmem_limit_bytes=VMEM_LIMIT),
    )(got, jnp.asarray(z_table))
    lines = lax.all_to_all(planes, "slab", split_axis=0, concat_axis=0, tiled=True)
    lines = lines.reshape(2, N_SLAB // 2, B_ROWS, KW)
    rows = T_BLOCK * X3
    return pl.pallas_call(
        line_kernel,
        name="line",
        out_shape=jax.ShapeDtypeStruct((2, X_OWN, NZ // N_SLAB, NY), jnp.float32),
        grid=(8 // T_BLOCK,),
        in_specs=[
            pl.BlockSpec((2, T_BLOCK, B_ROWS, KW), lambda i: (0, i, 0, 0)),
            whole,
        ],
        out_specs=pl.BlockSpec((2, rows, NZ // N_SLAB, NY), lambda i: (0, i, 0, 0)),
        scratch_shapes=[pltpu.VMEM((4, rows * 32, 768), jnp.bfloat16)],
        compiler_params=params,
    )(lines, jnp.asarray(y_table))


def solution(mesh):
    in_specs = (
        P(("half", "slab", "img"), None, None, None),
        P(),
        P(("half", "slab", "img"), None),
        P(("half", "slab", "img")),
        P(("half", "slab", "img")),
    )
    out_specs = P(None, ("half", "img"), "slab", None)
    return jax.shard_map(
        per_device, mesh=mesh, in_specs=in_specs, out_specs=out_specs, check_vma=False
    )
```

```python
import functools
import math

import jax
import jax.numpy as jnp
import ml_dtypes
import numpy as np
from jax import lax
from jax.experimental import pallas as pl
from jax.experimental.pallas import tpu as pltpu
from jax.sharding import PartitionSpec as P

NY = 512
NZ = 512
KW = 128
N_SLAB = 16
N_IMG = 4
N_DEST = N_SLAB * N_IMG
ITEMS = 64
XW = 96
X_OWN = XW // N_IMG
X3 = 3
ROWS = 2 * XW
Q = 2 * X3
A_ROWS = Q * 32 + 8
B_ROWS = 2 * Q * 32 + 8
PITCH = 33
LEVEL = 32700.0
TINY = 1e-30
STEP_ITEMS = 16
ITEM_STEPS = ITEMS // STEP_ITEMS
STEP_DESTS = 16
UNROLL = 8
T_BLOCK = 2
SPREAD_VMEM = 60 * 1024 * 1024
VMEM_LIMIT = 28 * 1024 * 1024


def split_bf16(values):
    high = values.astype(ml_dtypes.bfloat16)
    low = (values - high.astype(np.float64)).astype(ml_dtypes.bfloat16)
    return high, low


def y_orders():
    lane = np.arange(KW)
    order = {}
    for pair in range(2):
        a, b, c, d = (0, 1, 2, 3) if pair == 0 else (1, 0, 3, 2)
        for b1, runs in enumerate(((a, c, b, d), (c, a, d, b))):
            order[pair, b1] = np.concatenate([4 * np.arange(32) + r for r in runs])
    y = {key: (2 * key[0] + key[1]) * KW + j for key, j in order.items()}
    near = (lane & 32) == 0
    first = [np.where(near, y[p, 0], y[p, 1]) for p in range(2)]
    second = [np.where(near, y[p, 1], y[p, 0]) for p in range(2)]
    low = lane < 64
    tiles = [
        np.where(low, first[0], first[1]),
        np.where(low, first[1], first[0]),
        np.where(low, second[0], second[1]),
        np.where(low, second[1], second[0]),
    ]
    for rho in range(4):
        assert np.all(tiles[rho] % 4 == rho)
    return order, tiles


@functools.lru_cache(None)
def constants():
    order, tiles = y_orders()
    lanes = np.stack([order[b // 2, b % 2] for b in (0, 1, 2, 3, 0, 1, 2, 3)]).astype(np.int32)
    k = np.arange(128)
    z_tables, y_tables = [], []
    for rho in range(4):
        factor = np.exp(2j * np.pi * (np.outer(k, 4 * k + rho) % NZ) / NZ)
        high, low = split_bf16(
            np.block([[factor.real, -factor.imag], [factor.imag, factor.real]])
        )
        z_tables.append(np.concatenate([high, low], axis=1))
        factor = np.exp(2j * np.pi * (np.outer(tiles[rho], k) % NY) / NY) / math.sqrt(NY * NZ)
        high, low = split_bf16(
            np.block([[factor.real, factor.imag], [-factor.imag, factor.real]])
        )
        y_tables.append(np.concatenate([high, low], axis=0))
    return lanes, np.stack(z_tables), np.stack(y_tables)


def dot(a, b):
    return jnp.dot(a, b, preferred_element_type=jnp.float32)


def halves(value):
    high = value.astype(jnp.bfloat16)
    return high, (value - high.astype(jnp.float32)).astype(jnp.bfloat16)


def scale_codes(largest):
    return jnp.ceil(jnp.log2(jnp.maximum(largest, TINY)) * 256.0)


def to_codes(value, inverse):
    return jnp.round(value * inverse).astype(jnp.int32).astype(jnp.int16)


def from_codes(codes):
    return codes.astype(jnp.int32).astype(jnp.float32)


def decode(ref, lead, base, rows, scale):
    parts = [
        from_codes(ref[(*lead, slice(at, at + 8), slice(None))]) * scale
        for at in range(base, base + rows, 8)
    ]
    return jnp.concatenate(parts, axis=0)


def scales_of(tail):
    return jnp.exp2(tail * (1.0 / 256.0)) * (1.0 / LEVEL)


def radix_4(re, im):
    sr, dr, tr, er = re[0] + re[2], re[0] - re[2], re[1] + re[3], re[1] - re[3]
    si, di, ti, ei = im[0] + im[2], im[0] - im[2], im[1] + im[3], im[1] - im[3]
    return (sr + tr, si + ti), (dr - ei, di + er), (sr - tr, si - ti), (dr + ei, di - er)


def spread_kernel(
    dest_s, plane_s, kid_s, samples_ref, kernels_ref, order_ref, out_ref, rows_ref, label_ref
):
    step = pl.program_id(0)
    lane = lax.broadcasted_iota(jnp.int32, (1, KW), 1)

    @pl.when(step == 0)
    def _():
        label_ref[...] = jnp.zeros_like(label_ref)

    @pl.when(step < ITEM_STEPS)
    def _():
        for u in range(STEP_ITEMS):
            item = step * STEP_ITEMS + u
            block = u % 4
            pair, b1 = block // 2, block % 2
            g = step * (STEP_ITEMS // 4) + u // 4
            table = kernels_ref[kid_s[item]].astype(jnp.float32)
            order = jnp.broadcast_to(order_ref[block : block + 1, :], (KW, KW))
            table = jnp.take_along_axis(table, order, axis=1, mode="promise_in_bounds")
            value = dot(samples_ref[u].reshape(ROWS, KW), table.astype(jnp.bfloat16))
            rows_ref[pl.ds(pair * ROWS * PITCH + b1 * 16 + g, ROWS, stride=PITCH), :] = value
            d = dest_s[item]
            flipped = ((d & 1) << 3) | ((d & 2) << 1) | ((d & 4) >> 1) | ((d & 8) >> 3)
            plane = plane_s[item] * 16 + flipped
            place = (plane & 3) * 128 + (plane >> 2)
            row = 8 * pair + 6 + b1
            label_ref[row : row + 1, :] = jnp.where(
                (lane & 15) == g, place, label_ref[row : row + 1, :]
            )

    @pl.when(step >= ITEM_STEPS)
    def _():
        sub = lax.broadcasted_iota(jnp.int32, (8, KW), 0)

        def one(n, carry):
            d = (step - ITEM_STEPS) * STEP_DESTS + n
            pair = (d % N_SLAB) // 8
            first = pair * ROWS + X_OWN * (d // N_SLAB) + X3 * (d % 8)
            values, tops = [], []
            for r in range(2):
                for x3 in range(X3):
                    value = rows_ref[pl.ds((first + r * XW + x3) * PITCH, 32), :]
                    values.append(value)
                    tops.append(jnp.max(jnp.abs(value), axis=0, keepdims=True))
            codes = scale_codes(jnp.concatenate(tops + [tops[0], tops[0]], axis=0))
            inverse = jnp.exp2(codes * (-1.0 / 256.0)) * LEVEL
            for q in range(Q):
                out_ref[n, q * 32 : (q + 1) * 32, :] = to_codes(values[q], inverse[q : q + 1])
            labels = label_ref[pl.ds(pl.multiple_of(pair * 8, 8), 8), :]
            tail = jnp.where(sub < Q, codes.astype(jnp.int32), labels)
            out_ref[n, Q * 32 : A_ROWS, :] = tail.astype(jnp.int16)
            return carry

        lax.fori_loop(0, STEP_DESTS, one, 0, unroll=UNROLL)


def plane_kernel(got_ref, w_ref, out_ref, hot_ref, x_ref, freq_ref, scale_ref):
    lane = lax.broadcasted_iota(jnp.int32, (1, KW), 1)
    place = lax.broadcasted_iota(jnp.int32, (NZ, KW), 0).astype(jnp.int16)
    one, zero = jnp.ones((), jnp.bfloat16), jnp.zeros((), jnp.bfloat16)
    near = (lane & 32) == 0
    for group in range(8):
        rows = [jnp.zeros((1, KW), jnp.int32), jnp.zeros((1, KW), jnp.int32)]
        for e in range(8):
            src = group * 8 + e
            tail = got_ref[src, Q * 32 : A_ROWS, :].astype(jnp.int32)
            scale_ref[src] = scales_of(tail.astype(jnp.float32))
            for b1 in range(2):
                rows[b1] = jnp.where((lane >> 4) == e, tail[6 + b1 : 7 + b1], rows[b1])
        for b1 in range(2):
            hit = jnp.where(place == rows[b1].astype(jnp.int16), one, zero)
            hot_ref[b1, :, group * KW : (group + 1) * KW] = hit
    codes_of = [[[None] * 2 for _ in range(X3)] for _ in range(N_SLAB)]
    for x3 in range(X3):
        for src in range(N_DEST):
            for r in range(2):
                q = r * X3 + x3
                for b1 in range(2):
                    base = q * 32 + b1 * 16
                    value = decode(got_ref, (src,), base, 16, scale_ref[src, q : q + 1, :])
                    high, low = halves(value)
                    x_ref[x3, b1, src * 16 : src * 16 + 16, r * KW : (r + 1) * KW] = high
                    x_ref[x3, b1, 1024 + src * 16 : 1040 + src * 16, r * KW : (r + 1) * KW] = low
        grid = [
            dot(jnp.concatenate([hot_ref[b1]] * 2, axis=1), x_ref[x3, b1])
            for b1 in range(2)
        ]
        for rho in range(4):
            at = slice(rho * 128, (rho + 1) * 128)
            parts = []
            for r in range(2):
                cols = slice(r * KW, (r + 1) * KW)
                t0, t1 = grid[0][at, cols], grid[1][at, cols]
                parts.append(
                    jnp.concatenate([jnp.where(near, t0, t1), jnp.where(near, t1, t0)], axis=1)
                )
            high, low = halves(jnp.concatenate(parts, axis=0))
            table = w_ref[rho]
            table = jnp.concatenate([table[:, :256], table], axis=1)
            freq_ref[x3, rho] = dot(table, jnp.concatenate([high, low, high], axis=0))
        for kk in range(4):
            tops = [[], [], [], []]
            for tile in range(2):
                cols = slice(tile * KW, (tile + 1) * KW)
                at_re, at_im = slice(kk * 32, kk * 32 + 32), slice(128 + kk * 32, 160 + kk * 32)
                out = radix_4(
                    [freq_ref[x3, rho, at_re, cols] for rho in range(4)],
                    [freq_ref[x3, rho, at_im, cols] for rho in range(4)],
                )
                for a in range(4):
                    freq_ref[x3, a, at_re, cols] = out[a][0]
                    freq_ref[x3, a, at_im, cols] = out[a][1]
                    top = jnp.maximum(jnp.abs(out[a][0]), jnp.abs(out[a][1]))
                    tops[a].append(jnp.max(top, axis=0, keepdims=True))
            codes = scale_codes(jnp.concatenate(tops[0] + tops[1] + tops[2] + tops[3], axis=0))
            inverse = jnp.exp2(codes * (-1.0 / 256.0)) * LEVEL
            for a in range(4):
                for tile in range(2):
                    cols = slice(tile * KW, (tile + 1) * KW)
                    n = 2 * a + tile
                    codes_of[4 * a + kk][x3][tile] = codes[n : n + 1]
                    base = (x3 * 2 + tile) * 64
                    for c in range(2):
                        value = freq_ref[x3, a, c * 128 + kk * 32 : c * 128 + kk * 32 + 32, cols]
                        out_ref[4 * a + kk, base + c * 32 : base + c * 32 + 32, :] = to_codes(
                            value, inverse[n : n + 1]
                        )
    for s in range(N_SLAB):
        rows = [codes_of[s][x3][tile] for x3 in range(X3) for tile in range(2)]
        rows = jnp.concatenate(rows + rows[:2], axis=0)
        out_ref[s, 2 * Q * 32 : B_ROWS, :] = rows.astype(jnp.int32).astype(jnp.int16)


def line_kernel(got_ref, w_ref, out_ref, x_ref):
    low_half = lax.broadcasted_iota(jnp.int32, (1, KW), 1) < 64
    for t in range(T_BLOCK):
        scale = [scales_of(from_codes(got_ref[p, t, 2 * Q * 32 : B_ROWS, :])) for p in range(2)]
        for x3 in range(X3):
            row = (t * X3 + x3) * 32
            for tile in range(2):
                n = x3 * 2 + tile
                for c in range(2):
                    base = n * 64 + c * 32
                    v0, v1 = (
                        decode(got_ref, (p, t), base, 32, scale[p][n : n + 1]) for p in range(2)
                    )
                    for half in range(2):
                        value = jnp.where(low_half, v0, v1) if half == 0 else jnp.where(low_half, v1, v0)
                        high, low = halves(value)
                        rho = 2 * tile + half
                        for third, part in enumerate((high, low, high)):
                            col = third * 256 + c * KW
                            x_ref[rho, row : row + 32, col : col + KW] = part
    parts = []
    for rho in range(4):
        table = w_ref[rho]
        parts.append(dot(x_ref[rho], jnp.concatenate([table[:256], table], axis=0)))
    for row in range(T_BLOCK * X3):
        at = slice(row * 32, (row + 1) * 32)
        out = radix_4([p[at, :KW] for p in parts], [p[at, KW:] for p in parts])
        for a in range(4):
            for c in range(2):
                out_ref[c, row, :, a * KW : (a + 1) * KW] = out[a][c]


def per_device(samples, kernels, dest, plane_off, kernel_id):
    lanes, z_table, y_table = constants()
    params = pltpu.CompilerParams(
        dimension_semantics=("arbitrary",), vmem_limit_bytes=VMEM_LIMIT
    )
    whole = pl.BlockSpec(memory_space=pltpu.VMEM)
    packed = pl.pallas_call(
        spread_kernel,
        name="spread",
        out_shape=jax.ShapeDtypeStruct((N_DEST, A_ROWS, KW), jnp.int16),
        grid_spec=pltpu.PrefetchScalarGridSpec(
            num_scalar_prefetch=3,
            grid=(ITEM_STEPS + N_DEST // STEP_DESTS,),
            in_specs=[
                pl.BlockSpec(
                    (STEP_ITEMS, 2, XW, KW),
                    lambda i, *_: (jnp.minimum(i, ITEM_STEPS - 1), 0, 0, 0),
                ),
                whole,
                whole,
            ],
            out_specs=pl.BlockSpec(
                (STEP_DESTS, A_ROWS, KW), lambda i, *_: (jnp.maximum(i - ITEM_STEPS, 0), 0, 0)
            ),
            scratch_shapes=[
                pltpu.VMEM((2 * ROWS * PITCH, KW), jnp.float32),
                pltpu.VMEM((16, KW), jnp.int32),
            ],
        ),
        compiler_params=pltpu.CompilerParams(
            dimension_semantics=("arbitrary",), vmem_limit_bytes=SPREAD_VMEM
        ),
    )(dest.reshape(ITEMS), plane_off, kernel_id, samples, kernels, jnp.asarray(lanes))
    got = lax.all_to_all(packed, ("img", "slab"), split_axis=0, concat_axis=0, tiled=True)
    planes = pl.pallas_call(
        plane_kernel,
        name="plane",
        out_shape=jax.ShapeDtypeStruct((N_SLAB, B_ROWS, KW), jnp.int16),
        in_specs=[whole, whole],
        out_specs=whole,
        scratch_shapes=[
            pltpu.VMEM((2, NZ, 1024), jnp.bfloat16),
            pltpu.VMEM((X3, 2, 2048, 256), jnp.bfloat16),
            pltpu.VMEM((X3, 4, 256, 256), jnp.float32),
            pltpu.VMEM((N_DEST, 8, KW), jnp.float32),
        ],
        compiler_params=pltpu.CompilerParams(vmem_limit_bytes=VMEM_LIMIT),
    )(got, jnp.asarray(z_table))
    lines = lax.all_to_all(planes, "slab", split_axis=0, concat_axis=0, tiled=True)
    lines = lines.reshape(2, N_SLAB // 2, B_ROWS, KW)
    rows = T_BLOCK * X3
    return pl.pallas_call(
        line_kernel,
        name="line",
        out_shape=jax.ShapeDtypeStruct((2, X_OWN, NZ // N_SLAB, NY), jnp.float32),
        grid=(8 // T_BLOCK,),
        in_specs=[
            pl.BlockSpec((2, T_BLOCK, B_ROWS, KW), lambda i: (0, i, 0, 0)),
            whole,
        ],
        out_specs=pl.BlockSpec((2, rows, NZ // N_SLAB, NY), lambda i: (0, i, 0, 0)),
        scratch_shapes=[pltpu.VMEM((4, rows * 32, 768), jnp.bfloat16)],
        compiler_params=params,
    )(lines, jnp.asarray(y_table))


def solution(mesh):
    in_specs = (
        P(("half", "slab", "img"), None, None, None),
        P(),
        P(("half", "slab", "img"), None),
        P(("half", "slab", "img")),
        P(("half", "slab", "img")),
    )
    out_specs = P(None, ("half", "img"), "slab", None)
    return jax.shard_map(
        per_device, mesh=mesh, in_specs=in_specs, out_specs=out_specs, check_vma=False
    )
```

```python
import functools
import math

import jax
import jax.numpy as jnp
import ml_dtypes
import numpy as np
from jax import lax
from jax.experimental import pallas as pl
from jax.experimental.pallas import tpu as pltpu
from jax.sharding import PartitionSpec as P

NY = 512
NZ = 512
KW = 128
N_SLAB = 16
N_IMG = 4
N_DEST = N_SLAB * N_IMG
ITEMS = 64
XW = 96
X_OWN = XW // N_IMG
X3 = 3
ROWS = 2 * XW
Q = 2 * X3
A_ROWS = Q * 32 + 8
B_ROWS = 2 * Q * 32 + 8
PITCH = 33
LEVEL = 32700.0
TINY = 1e-30
STEP_ITEMS = 16
UNROLL = 8
T_BLOCK = 2
VMEM_LIMIT = 28 * 1024 * 1024


def split_bf16(values):
    high = values.astype(ml_dtypes.bfloat16)
    low = (values - high.astype(np.float64)).astype(ml_dtypes.bfloat16)
    return high, low


def y_orders():
    lane = np.arange(KW)
    order = {}
    for pair in range(2):
        a, b, c, d = (0, 1, 2, 3) if pair == 0 else (1, 0, 3, 2)
        for b1, runs in enumerate(((a, c, b, d), (c, a, d, b))):
            order[pair, b1] = np.concatenate([4 * np.arange(32) + r for r in runs])
    y = {key: (2 * key[0] + key[1]) * KW + j for key, j in order.items()}
    near = (lane & 32) == 0
    first = [np.where(near, y[p, 0], y[p, 1]) for p in range(2)]
    second = [np.where(near, y[p, 1], y[p, 0]) for p in range(2)]
    low = lane < 64
    tiles = [
        np.where(low, first[0], first[1]),
        np.where(low, first[1], first[0]),
        np.where(low, second[0], second[1]),
        np.where(low, second[1], second[0]),
    ]
    for rho in range(4):
        assert np.all(tiles[rho] % 4 == rho)
    return tiles


@functools.lru_cache(None)
def constants():
    tiles = y_orders()
    k = np.arange(128)
    z_tables, y_tables = [], []
    for rho in range(4):
        factor = np.exp(2j * np.pi * (np.outer(k, 4 * k + rho) % NZ) / NZ)
        high, low = split_bf16(
            np.block([[factor.real, -factor.imag], [factor.imag, factor.real]])
        )
        z_tables.append(np.concatenate([high, low], axis=1))
        factor = np.exp(2j * np.pi * (np.outer(tiles[rho], k) % NY) / NY) / math.sqrt(NY * NZ)
        high, low = split_bf16(
            np.block([[factor.real, factor.imag], [-factor.imag, factor.real]])
        )
        y_tables.append(np.concatenate([high, low], axis=0))
    return np.stack(z_tables), np.stack(y_tables)


def dot(a, b):
    return jnp.dot(a, b, preferred_element_type=jnp.float32)


def halves(value):
    high = value.astype(jnp.bfloat16)
    return high, (value - high.astype(jnp.float32)).astype(jnp.bfloat16)


def scale_codes(largest):
    return jnp.ceil(jnp.log2(jnp.maximum(largest, TINY)) * 256.0)


def to_codes(value, inverse):
    return jnp.round(value * inverse).astype(jnp.int32).astype(jnp.int16)


def from_codes(codes):
    return codes.astype(jnp.int32).astype(jnp.float32)


def decode(ref, lead, base, rows, scale):
    parts = [
        from_codes(ref[(*lead, slice(at, at + 8), slice(None))]) * scale
        for at in range(base, base + rows, 8)
    ]
    return jnp.concatenate(parts, axis=0)


def scales_of(tail):
    return jnp.exp2(tail * (1.0 / 256.0)) * (1.0 / LEVEL)


def radix_4(re, im):
    sr, dr, tr, er = re[0] + re[2], re[0] - re[2], re[1] + re[3], re[1] - re[3]
    si, di, ti, ei = im[0] + im[2], im[0] - im[2], im[1] + im[3], im[1] - im[3]
    return (sr + tr, si + ti), (dr - ei, di + er), (sr - tr, si - ti), (dr + ei, di - er)


def spread_kernel(
    dest_hbm, plane_hbm, kid_hbm, samples_hbm, kernels_hbm, out_ref,
    dest_s, plane_s, kid_s, samples_ref, kernels_ref, rows_ref, label_ref,
    index_sem, samples_sem, kernels_sem,
):
    lane = lax.broadcasted_iota(jnp.int32, (1, KW), 1)
    sub = lax.broadcasted_iota(jnp.int32, (8, KW), 0)

    def samples_copy(step):
        at = pl.ds(step * STEP_ITEMS, STEP_ITEMS)
        return pltpu.make_async_copy(samples_hbm.at[at], samples_ref.at[at], samples_sem.at[step])

    def kernel_copy(step, item):
        return pltpu.make_async_copy(
            kernels_hbm.at[kid_s[item]], kernels_ref.at[item], kernels_sem.at[step]
        )

    def kernels_wait(step):
        at = pl.ds(step * STEP_ITEMS, STEP_ITEMS)
        pltpu.make_async_copy(
            kernels_hbm.at[pl.ds(0, STEP_ITEMS)], kernels_ref.at[at], kernels_sem.at[step]
        ).wait()

    index_copies = [
        pltpu.make_async_copy(src, dst, index_sem.at[n])
        for n, (src, dst) in enumerate(
            ((kid_hbm, kid_s), (dest_hbm, dest_s), (plane_hbm, plane_s))
        )
    ]
    for copy in index_copies:
        copy.start()
    samples_copy(0).start()
    label_ref[...] = jnp.zeros_like(label_ref)
    run, within = lane >> 5, lane & 31
    orders = [
        jnp.broadcast_to(4 * within + 2 * ((run & 1) ^ b1) + ((run >> 1) ^ pair), (KW, KW))
        for pair in range(2)
        for b1 in range(2)
    ]
    index_copies[0].wait()
    for step in range(ITEMS // STEP_ITEMS):
        if step > 0:
            samples_copy(step).start()
        for u in range(STEP_ITEMS):
            kernel_copy(step, step * STEP_ITEMS + u).start()
    for copy in index_copies[1:]:
        copy.wait()

    def multiply(step, carry):
        samples_copy(step).wait()
        kernels_wait(step)
        for u in range(STEP_ITEMS):
            item = step * STEP_ITEMS + u
            block = u % 4
            pair, b1 = block // 2, block % 2
            g = step * (STEP_ITEMS // 4) + u // 4
            table = kernels_ref[item].astype(jnp.float32)
            table = jnp.take_along_axis(table, orders[block], axis=1, mode="promise_in_bounds")
            value = dot(samples_ref[item].reshape(ROWS, KW), table.astype(jnp.bfloat16))
            rows_ref[pl.ds(pair * ROWS * PITCH + b1 * 16 + g, ROWS, stride=PITCH), :] = value
            d = dest_s[item]
            flipped = ((d & 1) << 3) | ((d & 2) << 1) | ((d & 4) >> 1) | ((d & 8) >> 3)
            plane = plane_s[item] * 16 + flipped
            place = (plane & 3) * 128 + (plane >> 2)
            row = 8 * pair + 6 + b1
            label_ref[row : row + 1, :] = jnp.where(
                (lane & 15) == g, place, label_ref[row : row + 1, :]
            )
        return carry

    lax.fori_loop(0, ITEMS // STEP_ITEMS, multiply, 0)

    def encode(d, carry):
        pair = (d % N_SLAB) // 8
        first = pair * ROWS + X_OWN * (d // N_SLAB) + X3 * (d % 8)
        values, tops = [], []
        for r in range(2):
            for x3 in range(X3):
                value = rows_ref[pl.ds((first + r * XW + x3) * PITCH, 32), :]
                values.append(value)
                tops.append(jnp.max(jnp.abs(value), axis=0, keepdims=True))
        codes = scale_codes(jnp.concatenate(tops + [tops[0], tops[0]], axis=0))
        inverse = jnp.exp2(codes * (-1.0 / 256.0)) * LEVEL
        for q in range(Q):
            out_ref[d, q * 32 : (q + 1) * 32, :] = to_codes(values[q], inverse[q : q + 1])
        labels = label_ref[pl.ds(pl.multiple_of(pair * 8, 8), 8), :]
        tail = jnp.where(sub < Q, codes.astype(jnp.int32), labels)
        out_ref[d, Q * 32 : A_ROWS, :] = tail.astype(jnp.int16)
        return carry

    lax.fori_loop(0, N_DEST, encode, 0, unroll=UNROLL)


def plane_kernel(got_ref, w_ref, out_ref, hot_ref, x_ref, freq_ref, scale_ref):
    lane = lax.broadcasted_iota(jnp.int32, (1, KW), 1)
    place = lax.broadcasted_iota(jnp.int32, (NZ, KW), 0).astype(jnp.int16)
    one, zero = jnp.ones((), jnp.bfloat16), jnp.zeros((), jnp.bfloat16)
    near = (lane & 32) == 0
    for group in range(8):
        rows = [jnp.zeros((1, KW), jnp.int32), jnp.zeros((1, KW), jnp.int32)]
        for e in range(8):
            src = group * 8 + e
            tail = got_ref[src, Q * 32 : A_ROWS, :].astype(jnp.int32)
            scale_ref[src] = scales_of(tail.astype(jnp.float32))
            for b1 in range(2):
                rows[b1] = jnp.where((lane >> 4) == e, tail[6 + b1 : 7 + b1], rows[b1])
        for b1 in range(2):
            hit = jnp.where(place == rows[b1].astype(jnp.int16), one, zero)
            hot_ref[b1, :, group * KW : (group + 1) * KW] = hit
    codes_of = [[[None] * 2 for _ in range(X3)] for _ in range(N_SLAB)]
    for x3 in range(X3):
        for src in range(N_DEST):
            for r in range(2):
                q = r * X3 + x3
                for b1 in range(2):
                    base = q * 32 + b1 * 16
                    value = decode(got_ref, (src,), base, 16, scale_ref[src, q : q + 1, :])
                    high, low = halves(value)
                    x_ref[x3, b1, src * 16 : src * 16 + 16, r * KW : (r + 1) * KW] = high
                    x_ref[x3, b1, 1024 + src * 16 : 1040 + src * 16, r * KW : (r + 1) * KW] = low
        grid = [
            dot(jnp.concatenate([hot_ref[b1]] * 2, axis=1), x_ref[x3, b1])
            for b1 in range(2)
        ]
        for rho in range(4):
            at = slice(rho * 128, (rho + 1) * 128)
            parts = []
            for r in range(2):
                cols = slice(r * KW, (r + 1) * KW)
                t0, t1 = grid[0][at, cols], grid[1][at, cols]
                parts.append(
                    jnp.concatenate([jnp.where(near, t0, t1), jnp.where(near, t1, t0)], axis=1)
                )
            high, low = halves(jnp.concatenate(parts, axis=0))
            table = w_ref[rho]
            table = jnp.concatenate([table[:, :256], table], axis=1)
            freq_ref[x3, rho] = dot(table, jnp.concatenate([high, low, high], axis=0))
        for kk in range(4):
            tops = [[], [], [], []]
            for tile in range(2):
                cols = slice(tile * KW, (tile + 1) * KW)
                at_re, at_im = slice(kk * 32, kk * 32 + 32), slice(128 + kk * 32, 160 + kk * 32)
                out = radix_4(
                    [freq_ref[x3, rho, at_re, cols] for rho in range(4)],
                    [freq_ref[x3, rho, at_im, cols] for rho in range(4)],
                )
                for a in range(4):
                    freq_ref[x3, a, at_re, cols] = out[a][0]
                    freq_ref[x3, a, at_im, cols] = out[a][1]
                    top = jnp.maximum(jnp.abs(out[a][0]), jnp.abs(out[a][1]))
                    tops[a].append(jnp.max(top, axis=0, keepdims=True))
            codes = scale_codes(jnp.concatenate(tops[0] + tops[1] + tops[2] + tops[3], axis=0))
            inverse = jnp.exp2(codes * (-1.0 / 256.0)) * LEVEL
            for a in range(4):
                for tile in range(2):
                    cols = slice(tile * KW, (tile + 1) * KW)
                    n = 2 * a + tile
                    codes_of[4 * a + kk][x3][tile] = codes[n : n + 1]
                    base = (x3 * 2 + tile) * 64
                    for c in range(2):
                        value = freq_ref[x3, a, c * 128 + kk * 32 : c * 128 + kk * 32 + 32, cols]
                        out_ref[4 * a + kk, base + c * 32 : base + c * 32 + 32, :] = to_codes(
                            value, inverse[n : n + 1]
                        )
    for s in range(N_SLAB):
        rows = [codes_of[s][x3][tile] for x3 in range(X3) for tile in range(2)]
        rows = jnp.concatenate(rows + rows[:2], axis=0)
        out_ref[s, 2 * Q * 32 : B_ROWS, :] = rows.astype(jnp.int32).astype(jnp.int16)


def line_kernel(got_ref, w_ref, out_ref, x_ref):
    first = pl.program_id(0) * T_BLOCK
    low_half = lax.broadcasted_iota(jnp.int32, (1, KW), 1) < 64
    for t in range(T_BLOCK):
        scale = [
            scales_of(from_codes(got_ref[p, first + t, 2 * Q * 32 : B_ROWS, :])) for p in range(2)
        ]
        for x3 in range(X3):
            row = (t * X3 + x3) * 32
            for tile in range(2):
                n = x3 * 2 + tile
                for c in range(2):
                    base = n * 64 + c * 32
                    v0, v1 = (
                        decode(got_ref, (p, first + t), base, 32, scale[p][n : n + 1])
                        for p in range(2)
                    )
                    for half in range(2):
                        value = jnp.where(low_half, v0, v1) if half == 0 else jnp.where(low_half, v1, v0)
                        high, low = halves(value)
                        rho = 2 * tile + half
                        for third, part in enumerate((high, low, high)):
                            col = third * 256 + c * KW
                            x_ref[rho, row : row + 32, col : col + KW] = part
    parts = []
    for rho in range(4):
        table = w_ref[rho]
        parts.append(dot(x_ref[rho], jnp.concatenate([table[:256], table], axis=0)))
    for row in range(T_BLOCK * X3):
        at = slice(row * 32, (row + 1) * 32)
        out = radix_4([p[at, :KW] for p in parts], [p[at, KW:] for p in parts])
        for a in range(4):
            for c in range(2):
                out_ref[c, row, :, a * KW : (a + 1) * KW] = out[a][c]


def per_device(samples, kernels, dest, plane_off, kernel_id):
    z_table, y_table = constants()
    params = pltpu.CompilerParams(
        dimension_semantics=("arbitrary",), vmem_limit_bytes=VMEM_LIMIT
    )
    whole = pl.BlockSpec(memory_space=pltpu.VMEM)
    sources = [dest.reshape(ITEMS), plane_off, kernel_id, samples, kernels]
    packed = pl.pallas_call(
        spread_kernel,
        name="spread",
        out_shape=jax.ShapeDtypeStruct((N_DEST, A_ROWS, KW), jnp.int16),
        in_specs=[pl.BlockSpec(memory_space=pltpu.HBM)] * 5,
        out_specs=whole,
        scratch_shapes=[
            pltpu.SMEM((ITEMS,), jnp.int32),
            pltpu.SMEM((ITEMS,), jnp.int32),
            pltpu.SMEM((ITEMS,), jnp.int32),
            pltpu.VMEM((ITEMS, 2, XW, KW), jnp.bfloat16),
            pltpu.VMEM((ITEMS, KW, KW), jnp.bfloat16),
            pltpu.VMEM((2 * ROWS * PITCH, KW), jnp.float32),
            pltpu.VMEM((16, KW), jnp.int32),
            pltpu.SemaphoreType.DMA((3,)),
            pltpu.SemaphoreType.DMA((ITEMS // STEP_ITEMS,)),
            pltpu.SemaphoreType.DMA((ITEMS // STEP_ITEMS,)),
        ],
        compiler_params=pltpu.CompilerParams(vmem_limit_bytes=VMEM_LIMIT),
    )(*[pltpu.with_memory_space_constraint(source, pltpu.HBM) for source in sources])
    got = lax.all_to_all(packed, ("img", "slab"), split_axis=0, concat_axis=0, tiled=True)
    planes = pl.pallas_call(
        plane_kernel,
        name="plane",
        out_shape=jax.ShapeDtypeStruct((N_SLAB, B_ROWS, KW), jnp.int16),
        in_specs=[whole, whole],
        out_specs=whole,
        scratch_shapes=[
            pltpu.VMEM((2, NZ, 1024), jnp.bfloat16),
            pltpu.VMEM((X3, 2, 2048, 256), jnp.bfloat16),
            pltpu.VMEM((X3, 4, 256, 256), jnp.float32),
            pltpu.VMEM((N_DEST, 8, KW), jnp.float32),
        ],
        compiler_params=pltpu.CompilerParams(vmem_limit_bytes=VMEM_LIMIT),
    )(got, jnp.asarray(z_table))
    lines = lax.all_to_all(planes, "slab", split_axis=0, concat_axis=0, tiled=True)
    lines = lines.reshape(2, N_SLAB // 2, B_ROWS, KW)
    rows = T_BLOCK * X3
    return pl.pallas_call(
        line_kernel,
        name="line",
        out_shape=jax.ShapeDtypeStruct((2, X_OWN, NZ // N_SLAB, NY), jnp.float32),
        grid=(8 // T_BLOCK,),
        in_specs=[
            whole,
            whole,
        ],
        out_specs=pl.BlockSpec((2, rows, NZ // N_SLAB, NY), lambda i: (0, i, 0, 0)),
        scratch_shapes=[pltpu.VMEM((4, rows * 32, 768), jnp.bfloat16)],
        compiler_params=params,
    )(lines, jnp.asarray(y_table))


def solution(mesh):
    in_specs = (
        P(("half", "slab", "img"), None, None, None),
        P(),
        P(("half", "slab", "img"), None),
        P(("half", "slab", "img")),
        P(("half", "slab", "img")),
    )
    out_specs = P(None, ("half", "img"), "slab", None)
    return jax.shard_map(
        per_device, mesh=mesh, in_specs=in_specs, out_specs=out_specs, check_vma=False
    )
```

```python
import functools
import math

import jax
import jax.numpy as jnp
import ml_dtypes
import numpy as np
from jax import lax
from jax.experimental import pallas as pl
from jax.experimental.pallas import tpu as pltpu
from jax.sharding import PartitionSpec as P

NY = 512
NZ = 512
KW = 128
N_SLAB = 16
N_IMG = 4
N_DEST = N_SLAB * N_IMG
ITEMS = 64
XW = 96
X_OWN = XW // N_IMG
X3 = 3
ROWS = 2 * XW
Q = 2 * X3
A_ROWS = Q * 32 + 8
B_ROWS = 2 * Q * 32 + 8
PITCH = 33
LEVEL = 32700.0
TINY = 1e-30
STEP_ITEMS = 16
UNROLL = 16
T_BLOCK = 2
VMEM_LIMIT = 28 * 1024 * 1024


def split_bf16(values):
    high = values.astype(ml_dtypes.bfloat16)
    low = (values - high.astype(np.float64)).astype(ml_dtypes.bfloat16)
    return high, low


def y_orders():
    lane = np.arange(KW)
    order = {}
    for pair in range(2):
        a, b, c, d = (0, 1, 2, 3) if pair == 0 else (1, 0, 3, 2)
        for b1, runs in enumerate(((a, c, b, d), (c, a, d, b))):
            order[pair, b1] = np.concatenate([4 * np.arange(32) + r for r in runs])
    y = {key: (2 * key[0] + key[1]) * KW + j for key, j in order.items()}
    near = (lane & 32) == 0
    first = [np.where(near, y[p, 0], y[p, 1]) for p in range(2)]
    second = [np.where(near, y[p, 1], y[p, 0]) for p in range(2)]
    low = lane < 64
    tiles = [
        np.where(low, first[0], first[1]),
        np.where(low, first[1], first[0]),
        np.where(low, second[0], second[1]),
        np.where(low, second[1], second[0]),
    ]
    for rho in range(4):
        assert np.all(tiles[rho] % 4 == rho)
    return tiles


@functools.lru_cache(None)
def constants():
    tiles = y_orders()
    k = np.arange(128)
    z_tables, y_tables = [], []
    for rho in range(4):
        factor = np.exp(2j * np.pi * (np.outer(k, 4 * k + rho) % NZ) / NZ)
        high, low = split_bf16(
            np.block([[factor.real, -factor.imag], [factor.imag, factor.real]])
        )
        z_tables.append(np.stack([t[:, n : n + KW] for t in (high, low) for n in (0, KW)]))
        factor = np.exp(2j * np.pi * (np.outer(tiles[rho], k) % NY) / NY) / math.sqrt(NY * NZ)
        high, low = split_bf16(
            np.block([[factor.real, factor.imag], [-factor.imag, factor.real]])
        )
        y_tables.append(np.concatenate([high, low], axis=0))
    return np.stack(z_tables), np.stack(y_tables)


def dot(a, b):
    return jnp.dot(a, b, preferred_element_type=jnp.float32)


def halves(value):
    high = value.astype(jnp.bfloat16)
    return high, (value - high.astype(jnp.float32)).astype(jnp.bfloat16)


def scale_codes(largest):
    return jnp.ceil(jnp.log2(jnp.maximum(largest, TINY)) * 256.0)


def to_codes(value, inverse):
    return jnp.round(value * inverse).astype(jnp.int32).astype(jnp.int16)


def from_codes(codes):
    return codes.astype(jnp.int32).astype(jnp.float32)


def decode(ref, lead, base, rows, scale):
    parts = [
        from_codes(ref[(*lead, slice(at, at + 8), slice(None))]) * scale
        for at in range(base, base + rows, 8)
    ]
    return jnp.concatenate(parts, axis=0)


def scales_of(tail):
    return jnp.exp2(tail * (1.0 / 256.0)) * (1.0 / LEVEL)


def radix_4(re, im):
    sr, dr, tr, er = re[0] + re[2], re[0] - re[2], re[1] + re[3], re[1] - re[3]
    si, di, ti, ei = im[0] + im[2], im[0] - im[2], im[1] + im[3], im[1] - im[3]
    return (sr + tr, si + ti), (dr - ei, di + er), (sr - tr, si - ti), (dr + ei, di - er)


def spread_kernel(
    dest_hbm, plane_hbm, kid_hbm, samples_hbm, kernels_hbm, out_ref,
    dest_s, plane_s, kid_s, samples_ref, kernels_ref, table_ref, rows_ref, label_ref,
    index_sem, samples_sem, kernels_sem,
):
    lane = lax.broadcasted_iota(jnp.int32, (1, KW), 1)
    sub = lax.broadcasted_iota(jnp.int32, (8, KW), 0)

    def samples_copy(step):
        at = pl.ds(step * STEP_ITEMS, STEP_ITEMS)
        return pltpu.make_async_copy(samples_hbm.at[at], samples_ref.at[at], samples_sem.at[step])

    def kernel_copy(step, item):
        return pltpu.make_async_copy(
            kernels_hbm.at[kid_s[item]], kernels_ref.at[item], kernels_sem.at[step]
        )

    def kernels_wait(step):
        at = pl.ds(step * STEP_ITEMS, STEP_ITEMS)
        pltpu.make_async_copy(
            kernels_hbm.at[pl.ds(0, STEP_ITEMS)], kernels_ref.at[at], kernels_sem.at[step]
        ).wait()

    index_copies = [
        pltpu.make_async_copy(src, dst, index_sem.at[n])
        for n, (src, dst) in enumerate(
            ((kid_hbm, kid_s), (dest_hbm, dest_s), (plane_hbm, plane_s))
        )
    ]
    for copy in index_copies:
        copy.start()
    samples_copy(0).start()
    label_ref[...] = jnp.zeros_like(label_ref)
    run, within = lane >> 5, lane & 31
    orders = [
        jnp.broadcast_to(4 * within + 2 * ((run & 1) ^ b1) + ((run >> 1) ^ pair), (KW, KW))
        for pair in range(2)
        for b1 in range(2)
    ]
    index_copies[0].wait()
    for step in range(ITEMS // STEP_ITEMS):
        if step > 0:
            samples_copy(step).start()
        for u in range(STEP_ITEMS):
            kernel_copy(step, step * STEP_ITEMS + u).start()
    for copy in index_copies[1:]:
        copy.wait()

    def order_columns(step):
        for u in range(STEP_ITEMS):
            table = kernels_ref[step * STEP_ITEMS + u].astype(jnp.float32)
            table = jnp.take_along_axis(table, orders[u % 4], axis=1, mode="promise_in_bounds")
            table_ref[step % 2, u] = table.astype(jnp.bfloat16)

    kernels_wait(0)
    order_columns(0)
    steps = ITEMS // STEP_ITEMS
    for step in range(steps):
        samples_copy(step).wait()
        if step + 1 < steps:
            kernels_wait(step + 1)
        for u in range(STEP_ITEMS):
            item = step * STEP_ITEMS + u
            pair, b1 = u % 4 // 2, u % 2
            g = item // 4
            value = dot(samples_ref[item].reshape(ROWS, KW), table_ref[step % 2, u])
            rows_ref[pl.ds(pair * ROWS * PITCH + b1 * 16 + g, ROWS, stride=PITCH), :] = value
            d = dest_s[item]
            flipped = ((d & 1) << 3) | ((d & 2) << 1) | ((d & 4) >> 1) | ((d & 8) >> 3)
            plane = plane_s[item] * 16 + flipped
            place = (plane & 3) * 128 + (plane >> 2)
            row = 8 * pair + 6 + b1
            label_ref[row : row + 1, :] = jnp.where(
                (lane & 15) == g, place, label_ref[row : row + 1, :]
            )
        if step + 1 < steps:
            order_columns(step + 1)

    def encode(d, carry):
        pair = (d % N_SLAB) // 8
        first = pair * ROWS + X_OWN * (d // N_SLAB) + X3 * (d % 8)
        values, tops = [], []
        for r in range(2):
            for x3 in range(X3):
                value = rows_ref[pl.ds((first + r * XW + x3) * PITCH, 32), :]
                values.append(value)
                tops.append(jnp.max(jnp.abs(value), axis=0, keepdims=True))
        codes = scale_codes(jnp.concatenate(tops + [tops[0], tops[0]], axis=0))
        inverse = jnp.exp2(codes * (-1.0 / 256.0)) * LEVEL
        for q in range(Q):
            out_ref[d, q * 32 : (q + 1) * 32, :] = to_codes(values[q], inverse[q : q + 1])
        labels = label_ref[pl.ds(pl.multiple_of(pair * 8, 8), 8), :]
        tail = jnp.where(sub < Q, codes.astype(jnp.int32), labels)
        out_ref[d, Q * 32 : A_ROWS, :] = tail.astype(jnp.int16)
        return carry

    lax.fori_loop(0, N_DEST, encode, 0, unroll=UNROLL)


def plane_kernel(got_ref, w_ref, out_ref, hot_ref, x_ref, freq_ref, scale_ref):
    lane = lax.broadcasted_iota(jnp.int32, (1, KW), 1)
    place = lax.broadcasted_iota(jnp.int32, (NZ, KW), 0).astype(jnp.int16)
    one, zero = jnp.ones((), jnp.bfloat16), jnp.zeros((), jnp.bfloat16)
    near = (lane & 32) == 0
    for group in range(8):
        rows = [jnp.zeros((1, KW), jnp.int32), jnp.zeros((1, KW), jnp.int32)]
        for e in range(8):
            src = group * 8 + e
            tail = got_ref[src, Q * 32 : A_ROWS, :].astype(jnp.int32)
            scale_ref[src] = scales_of(tail.astype(jnp.float32))
            for b1 in range(2):
                rows[b1] = jnp.where((lane >> 4) == e, tail[6 + b1 : 7 + b1], rows[b1])
        for b1 in range(2):
            hit = jnp.where(place == rows[b1].astype(jnp.int16), one, zero)
            hot_ref[b1, group] = hit
    codes_of = [[[None] * 2 for _ in range(X3)] for _ in range(N_SLAB)]
    for x3 in range(X3):
        for src in range(N_DEST):
            for r in range(2):
                q = r * X3 + x3
                for b1 in range(2):
                    base = q * 32 + b1 * 16
                    value = decode(got_ref, (src,), base, 16, scale_ref[src, q : q + 1, :])
                    high, low = halves(value)
                    x_ref[x3, b1, r, src * 16 : src * 16 + 16, :] = high
                    x_ref[x3, b1, r, 1024 + src * 16 : 1040 + src * 16, :] = low
        grid = [
            dot(
                jnp.concatenate([hot_ref[b1, group] for group in range(8)] * 2, axis=1),
                jnp.concatenate([x_ref[x3, b1, r] for r in range(2)], axis=1),
            )
            for b1 in range(2)
        ]
        for rho in range(4):
            at = slice(rho * 128, (rho + 1) * 128)
            parts = []
            for r in range(2):
                cols = slice(r * KW, (r + 1) * KW)
                t0, t1 = grid[0][at, cols], grid[1][at, cols]
                parts.append(
                    jnp.concatenate([jnp.where(near, t0, t1), jnp.where(near, t1, t0)], axis=1)
                )
            high, low = halves(jnp.concatenate(parts, axis=0))
            table = jnp.concatenate([w_ref[rho, n] for n in (0, 1, 0, 1, 2, 3)], axis=1)
            freq_ref[x3, rho] = dot(table, jnp.concatenate([high, low, high], axis=0))
        for kk in range(4):
            tops = [[], [], [], []]
            for tile in range(2):
                cols = slice(tile * KW, (tile + 1) * KW)
                at_re, at_im = slice(kk * 32, kk * 32 + 32), slice(128 + kk * 32, 160 + kk * 32)
                out = radix_4(
                    [freq_ref[x3, rho, at_re, cols] for rho in range(4)],
                    [freq_ref[x3, rho, at_im, cols] for rho in range(4)],
                )
                for a in range(4):
                    freq_ref[x3, a, at_re, cols] = out[a][0]
                    freq_ref[x3, a, at_im, cols] = out[a][1]
                    top = jnp.maximum(jnp.abs(out[a][0]), jnp.abs(out[a][1]))
                    tops[a].append(jnp.max(top, axis=0, keepdims=True))
            codes = scale_codes(jnp.concatenate(tops[0] + tops[1] + tops[2] + tops[3], axis=0))
            inverse = jnp.exp2(codes * (-1.0 / 256.0)) * LEVEL
            for a in range(4):
                for tile in range(2):
                    cols = slice(tile * KW, (tile + 1) * KW)
                    n = 2 * a + tile
                    codes_of[4 * a + kk][x3][tile] = codes[n : n + 1]
                    base = (x3 * 2 + tile) * 64
                    for c in range(2):
                        value = freq_ref[x3, a, c * 128 + kk * 32 : c * 128 + kk * 32 + 32, cols]
                        out_ref[4 * a + kk, base + c * 32 : base + c * 32 + 32, :] = to_codes(
                            value, inverse[n : n + 1]
                        )
    for s in range(N_SLAB):
        rows = [codes_of[s][x3][tile] for x3 in range(X3) for tile in range(2)]
        rows = jnp.concatenate(rows + rows[:2], axis=0)
        out_ref[s, 2 * Q * 32 : B_ROWS, :] = rows.astype(jnp.int32).astype(jnp.int16)


def line_kernel(got_ref, w_ref, out_ref, x_ref):
    first = pl.program_id(0) * T_BLOCK
    low_half = lax.broadcasted_iota(jnp.int32, (1, KW), 1) < 64
    for t in range(T_BLOCK):
        scale = [
            scales_of(from_codes(got_ref[p, first + t, 2 * Q * 32 : B_ROWS, :])) for p in range(2)
        ]
        for x3 in range(X3):
            row = (t * X3 + x3) * 32
            for tile in range(2):
                n = x3 * 2 + tile
                for c in range(2):
                    base = n * 64 + c * 32
                    v0, v1 = (
                        decode(got_ref, (p, first + t), base, 32, scale[p][n : n + 1])
                        for p in range(2)
                    )
                    for half in range(2):
                        value = jnp.where(low_half, v0, v1) if half == 0 else jnp.where(low_half, v1, v0)
                        high, low = halves(value)
                        rho = 2 * tile + half
                        for third, part in enumerate((high, low)):
                            x_ref[rho, third * 2 + c, row : row + 32, :] = part
    parts = []
    for rho in range(4):
        table = w_ref[rho]
        lines = jnp.concatenate([x_ref[rho, n] for n in (0, 1, 2, 3, 0, 1)], axis=1)
        parts.append(dot(lines, jnp.concatenate([table[:256], table], axis=0)))
    for row in range(T_BLOCK * X3):
        at = slice(row * 32, (row + 1) * 32)
        out = radix_4([p[at, :KW] for p in parts], [p[at, KW:] for p in parts])
        for a in range(4):
            for c in range(2):
                out_ref[c, row, :, a * KW : (a + 1) * KW] = out[a][c]


def per_device(samples, kernels, dest, plane_off, kernel_id):
    z_table, y_table = constants()
    params = pltpu.CompilerParams(
        dimension_semantics=("arbitrary",), vmem_limit_bytes=VMEM_LIMIT
    )
    whole = pl.BlockSpec(memory_space=pltpu.VMEM)
    sources = [dest.reshape(ITEMS), plane_off, kernel_id, samples, kernels]
    packed = pl.pallas_call(
        spread_kernel,
        name="spread",
        out_shape=jax.ShapeDtypeStruct((N_DEST, A_ROWS, KW), jnp.int16),
        in_specs=[pl.BlockSpec(memory_space=pltpu.HBM)] * 5,
        out_specs=whole,
        scratch_shapes=[
            pltpu.SMEM((ITEMS,), jnp.int32),
            pltpu.SMEM((ITEMS,), jnp.int32),
            pltpu.SMEM((ITEMS,), jnp.int32),
            pltpu.VMEM((ITEMS, 2, XW, KW), jnp.bfloat16),
            pltpu.VMEM((ITEMS, KW, KW), jnp.bfloat16),
            pltpu.VMEM((2, STEP_ITEMS, KW, KW), jnp.bfloat16),
            pltpu.VMEM((2 * ROWS * PITCH, KW), jnp.float32),
            pltpu.VMEM((16, KW), jnp.int32),
            pltpu.SemaphoreType.DMA((3,)),
            pltpu.SemaphoreType.DMA((ITEMS // STEP_ITEMS,)),
            pltpu.SemaphoreType.DMA((ITEMS // STEP_ITEMS,)),
        ],
        compiler_params=pltpu.CompilerParams(vmem_limit_bytes=VMEM_LIMIT),
    )(*[pltpu.with_memory_space_constraint(source, pltpu.HBM) for source in sources])
    got = lax.all_to_all(packed, ("img", "slab"), split_axis=0, concat_axis=0, tiled=True)
    planes = pl.pallas_call(
        plane_kernel,
        name="plane",
        out_shape=jax.ShapeDtypeStruct((N_SLAB, B_ROWS, KW), jnp.int16),
        in_specs=[whole, whole],
        out_specs=whole,
        scratch_shapes=[
            pltpu.VMEM((2, 8, NZ, KW), jnp.bfloat16),
            pltpu.VMEM((X3, 2, 2, 2048, KW), jnp.bfloat16),
            pltpu.VMEM((X3, 4, 256, 256), jnp.float32),
            pltpu.VMEM((N_DEST, 8, KW), jnp.float32),
        ],
        compiler_params=pltpu.CompilerParams(vmem_limit_bytes=VMEM_LIMIT),
    )(got, jnp.asarray(z_table))
    lines = lax.all_to_all(planes, "slab", split_axis=0, concat_axis=0, tiled=True)
    lines = lines.reshape(2, N_SLAB // 2, B_ROWS, KW)
    rows = T_BLOCK * X3
    return pl.pallas_call(
        line_kernel,
        name="line",
        out_shape=jax.ShapeDtypeStruct((2, X_OWN, NZ // N_SLAB, NY), jnp.float32),
        grid=(8 // T_BLOCK,),
        in_specs=[
            whole,
            whole,
        ],
        out_specs=pl.BlockSpec((2, rows, NZ // N_SLAB, NY), lambda i: (0, i, 0, 0)),
        scratch_shapes=[pltpu.VMEM((4, 4, rows * 32, KW), jnp.bfloat16)],
        compiler_params=params,
    )(lines, jnp.asarray(y_table))


def solution(mesh):
    in_specs = (
        P(("half", "slab", "img"), None, None, None),
        P(),
        P(("half", "slab", "img"), None),
        P(("half", "slab", "img")),
        P(("half", "slab", "img")),
    )
    out_specs = P(None, ("half", "img"), "slab", None)
    return jax.shard_map(
        per_device, mesh=mesh, in_specs=in_specs, out_specs=out_specs, check_vma=False
    )
```

```python
import functools
import math

import jax
import jax.numpy as jnp
import ml_dtypes
import numpy as np
from jax import lax
from jax.experimental import pallas as pl
from jax.experimental.pallas import tpu as pltpu
from jax.sharding import PartitionSpec as P

NY = 512
NZ = 512
KW = 128
N_SLAB = 16
N_IMG = 4
N_DEST = N_SLAB * N_IMG
ITEMS = 64
XW = 96
X_OWN = XW // N_IMG
X3 = 3
ROWS = 2 * XW
Q = 2 * X3
A_ROWS = Q * 32 + 8
B_ROWS = 2 * Q * 32 + 8
PITCH = 33
LEVEL = 32700.0
TINY = 1e-30
STEP_ITEMS = 16
UNROLL = 16
T_BLOCK = 2
VMEM_LIMIT = 28 * 1024 * 1024


def flip(value, bits):
    total = value * 0
    for bit in range(bits):
        total = total | (((value >> bit) & 1) << (bits - 1 - bit))
    return total


def split_bf16(values):
    high = values.astype(ml_dtypes.bfloat16)
    low = (values - high.astype(np.float64)).astype(ml_dtypes.bfloat16)
    return high, low


def y_orders():
    lane = np.arange(KW)
    order = {}
    for pair in range(2):
        a, b, c, d = (0, 1, 2, 3) if pair == 0 else (1, 0, 3, 2)
        for b1, runs in enumerate(((a, c, b, d), (c, a, d, b))):
            order[pair, b1] = np.concatenate([4 * np.arange(32) + r for r in runs])
    y = {key: (2 * key[0] + key[1]) * KW + j for key, j in order.items()}
    near = (lane & 32) == 0
    first = [np.where(near, y[p, 0], y[p, 1]) for p in range(2)]
    second = [np.where(near, y[p, 1], y[p, 0]) for p in range(2)]
    low = lane < 64
    tiles = [
        np.where(low, first[0], first[1]),
        np.where(low, first[1], first[0]),
        np.where(low, second[0], second[1]),
        np.where(low, second[1], second[0]),
    ]
    for rho in range(4):
        assert np.all(tiles[rho] % 4 == rho)
    return tiles


@functools.lru_cache(None)
def constants():
    tiles = y_orders()
    k = np.arange(128)
    z_tables, y_tables = [], []
    for rho in range(4):
        factor = np.exp(2j * np.pi * (np.outer(k, 4 * k + rho) % NZ) / NZ)
        high, low = split_bf16(
            np.block([[factor.real, -factor.imag], [factor.imag, factor.real]])
        )
        z_tables.append(np.stack([t[:, n : n + KW] for t in (high, low) for n in (0, KW)]))
        factor = np.exp(2j * np.pi * (np.outer(tiles[rho], k) % NY) / NY) / math.sqrt(NY * NZ)
        high, low = split_bf16(
            np.block([[factor.real, factor.imag], [-factor.imag, factor.real]])
        )
        y_tables.append(np.concatenate([high, low], axis=0))
    return np.stack(z_tables), np.stack(y_tables)


def dot(a, b):
    return jnp.dot(a, b, preferred_element_type=jnp.float32)


def halves(value):
    high = value.astype(jnp.bfloat16)
    return high, (value - high.astype(jnp.float32)).astype(jnp.bfloat16)


def scale_codes(largest):
    return jnp.ceil(jnp.log2(jnp.maximum(largest, TINY)) * 256.0)


def to_codes(value, inverse):
    return jnp.round(value * inverse).astype(jnp.int32).astype(jnp.int16)


def from_codes(codes):
    return codes.astype(jnp.int32).astype(jnp.float32)


def decode(ref, lead, base, rows, scale):
    parts = [
        from_codes(ref[(*lead, slice(at, at + 8), slice(None))]) * scale
        for at in range(base, base + rows, 8)
    ]
    return jnp.concatenate(parts, axis=0)


def scales_of(tail):
    return jnp.exp2(tail * (1.0 / 256.0)) * (1.0 / LEVEL)


def radix_4(re, im):
    sr, dr, tr, er = re[0] + re[2], re[0] - re[2], re[1] + re[3], re[1] - re[3]
    si, di, ti, ei = im[0] + im[2], im[0] - im[2], im[1] + im[3], im[1] - im[3]
    return (sr + tr, si + ti), (dr - ei, di + er), (sr - tr, si - ti), (dr + ei, di - er)


def spread_kernel(
    dest_hbm, plane_hbm, kid_hbm, samples_hbm, kernels_hbm, out_ref,
    dest_s, plane_s, kid_s, samples_ref, kernels_ref, table_ref, rows_ref, label_ref,
    index_sem, samples_sem, kernels_sem,
):
    lane = lax.broadcasted_iota(jnp.int32, (1, KW), 1)
    sub = lax.broadcasted_iota(jnp.int32, (8, KW), 0)

    def samples_copy(step):
        at = pl.ds(step * STEP_ITEMS, STEP_ITEMS)
        return pltpu.make_async_copy(samples_hbm.at[at], samples_ref.at[at], samples_sem.at[step])

    def kernel_copy(step, item):
        return pltpu.make_async_copy(
            kernels_hbm.at[kid_s[item]], kernels_ref.at[item], kernels_sem.at[step]
        )

    def kernels_wait(step):
        at = pl.ds(step * STEP_ITEMS, STEP_ITEMS)
        pltpu.make_async_copy(
            kernels_hbm.at[pl.ds(0, STEP_ITEMS)], kernels_ref.at[at], kernels_sem.at[step]
        ).wait()

    index_copies = [
        pltpu.make_async_copy(src, dst, index_sem.at[n])
        for n, (src, dst) in enumerate(
            ((kid_hbm, kid_s), (dest_hbm, dest_s), (plane_hbm, plane_s))
        )
    ]
    for copy in index_copies:
        copy.start()
    samples_copy(0).start()
    label_ref[...] = jnp.zeros_like(label_ref)
    run, within = lane >> 5, lane & 31
    orders = [
        jnp.broadcast_to(4 * within + 2 * ((run & 1) ^ b1) + ((run >> 1) ^ pair), (KW, KW))
        for pair in range(2)
        for b1 in range(2)
    ]
    index_copies[0].wait()
    for step in range(ITEMS // STEP_ITEMS):
        if step > 0:
            samples_copy(step).start()
        for u in range(STEP_ITEMS):
            kernel_copy(step, step * STEP_ITEMS + u).start()
    for copy in index_copies[1:]:
        copy.wait()

    def order_columns(step):
        for u in range(STEP_ITEMS):
            table = kernels_ref[step * STEP_ITEMS + u].astype(jnp.float32)
            table = jnp.take_along_axis(table, orders[u % 4], axis=1, mode="promise_in_bounds")
            table_ref[step % 2, u] = table.astype(jnp.bfloat16)

    kernels_wait(0)
    order_columns(0)
    steps = ITEMS // STEP_ITEMS
    for step in range(steps):
        samples_copy(step).wait()
        if step + 1 < steps:
            kernels_wait(step + 1)
        for u in range(STEP_ITEMS):
            item = step * STEP_ITEMS + u
            pair, b1 = u % 4 // 2, u % 2
            g = item // 4
            value = dot(samples_ref[item].reshape(ROWS, KW), table_ref[step % 2, u])
            rows_ref[pl.ds(pair * ROWS * PITCH + b1 * 16 + g, ROWS, stride=PITCH), :] = value
            d = dest_s[item]
            flipped = ((d & 1) << 3) | ((d & 2) << 1) | ((d & 4) >> 1) | ((d & 8) >> 3)
            plane = plane_s[item] * 16 + flipped
            place = (plane & 3) * 128 + (plane >> 2)
            row = 8 * pair + 6 + b1
            label_ref[row : row + 1, :] = jnp.where(
                (lane & 15) == g, place, label_ref[row : row + 1, :]
            )
        if step + 1 < steps:
            order_columns(step + 1)

    def encode(d, carry):
        pair = (d % N_SLAB) // 8
        first = pair * ROWS + X_OWN * (d // N_SLAB) + X3 * (d % 8)
        values, tops = [], []
        for r in range(2):
            for x3 in range(X3):
                value = rows_ref[pl.ds((first + r * XW + x3) * PITCH, 32), :]
                values.append(value)
                tops.append(jnp.max(jnp.abs(value), axis=0, keepdims=True))
        codes = scale_codes(jnp.concatenate(tops + [tops[0], tops[0]], axis=0))
        inverse = jnp.exp2(codes * (-1.0 / 256.0)) * LEVEL
        for q in range(Q):
            out_ref[d, q * 32 : (q + 1) * 32, :] = to_codes(values[q], inverse[q : q + 1])
        labels = label_ref[pl.ds(pl.multiple_of(pair * 8, 8), 8), :]
        tail = jnp.where(sub < Q, codes.astype(jnp.int32), labels)
        out_ref[d, Q * 32 : A_ROWS, :] = tail.astype(jnp.int16)
        return carry

    lax.fori_loop(0, N_DEST, encode, 0, unroll=UNROLL)


def plane_kernel(got_ref, w_ref, out_ref, hot_ref, x_ref, freq_ref, scale_ref):
    lane = lax.broadcasted_iota(jnp.int32, (1, KW), 1)
    place = lax.broadcasted_iota(jnp.int32, (NZ, KW), 0).astype(jnp.int16)
    one, zero = jnp.ones((), jnp.bfloat16), jnp.zeros((), jnp.bfloat16)
    near = (lane & 32) == 0
    for group in range(8):
        rows = [jnp.zeros((1, KW), jnp.int32), jnp.zeros((1, KW), jnp.int32)]
        for e in range(8):
            src = group * 8 + e
            tail = got_ref[src, Q * 32 : A_ROWS, :].astype(jnp.int32)
            scale_ref[src] = scales_of(tail.astype(jnp.float32))
            for b1 in range(2):
                rows[b1] = jnp.where((lane >> 4) == e, tail[6 + b1 : 7 + b1], rows[b1])
        for b1 in range(2):
            hit = jnp.where(place == rows[b1].astype(jnp.int16), one, zero)
            hot_ref[b1, group] = hit
    codes_of = [[[None] * 2 for _ in range(X3)] for _ in range(N_SLAB)]
    for x3 in range(X3):
        for src in range(N_DEST):
            for r in range(2):
                q = r * X3 + x3
                for b1 in range(2):
                    base = q * 32 + b1 * 16
                    value = decode(got_ref, (src,), base, 16, scale_ref[src, q : q + 1, :])
                    high, low = halves(value)
                    x_ref[x3, b1, r, src * 16 : src * 16 + 16, :] = high
                    x_ref[x3, b1, r, 1024 + src * 16 : 1040 + src * 16, :] = low
        grid = [
            dot(
                jnp.concatenate([hot_ref[b1, group] for group in range(8)] * 2, axis=1),
                jnp.concatenate([x_ref[x3, b1, r] for r in range(2)], axis=1),
            )
            for b1 in range(2)
        ]
        for rho in range(4):
            at = slice(rho * 128, (rho + 1) * 128)
            parts = []
            for r in range(2):
                cols = slice(r * KW, (r + 1) * KW)
                t0, t1 = grid[0][at, cols], grid[1][at, cols]
                parts.append(
                    jnp.concatenate([jnp.where(near, t0, t1), jnp.where(near, t1, t0)], axis=1)
                )
            high, low = halves(jnp.concatenate(parts, axis=0))
            table = jnp.concatenate([w_ref[rho, n] for n in (0, 1, 0, 1, 2, 3)], axis=1)
            freq_ref[x3, rho] = dot(table, jnp.concatenate([high, low, high], axis=0))
        for kk in range(4):
            tops = [[], [], [], []]
            for tile in range(2):
                cols = slice(tile * KW, (tile + 1) * KW)
                at_re, at_im = slice(kk * 32, kk * 32 + 32), slice(128 + kk * 32, 160 + kk * 32)
                out = radix_4(
                    [freq_ref[x3, rho, at_re, cols] for rho in range(4)],
                    [freq_ref[x3, rho, at_im, cols] for rho in range(4)],
                )
                for a in range(4):
                    freq_ref[x3, a, at_re, cols] = out[a][0]
                    freq_ref[x3, a, at_im, cols] = out[a][1]
                    top = jnp.maximum(jnp.abs(out[a][0]), jnp.abs(out[a][1]))
                    tops[a].append(jnp.max(top, axis=0, keepdims=True))
            codes = scale_codes(jnp.concatenate(tops[0] + tops[1] + tops[2] + tops[3], axis=0))
            inverse = jnp.exp2(codes * (-1.0 / 256.0)) * LEVEL
            for a in range(4):
                for tile in range(2):
                    cols = slice(tile * KW, (tile + 1) * KW)
                    n = 2 * a + tile
                    codes_of[4 * a + kk][x3][tile] = codes[n : n + 1]
                    base = (x3 * 2 + tile) * 64
                    for c in range(2):
                        value = freq_ref[x3, a, c * 128 + kk * 32 : c * 128 + kk * 32 + 32, cols]
                        out_ref[flip(4 * a + kk, 4), base + c * 32 : base + c * 32 + 32, :] = to_codes(
                            value, inverse[n : n + 1]
                        )
    for s in range(N_SLAB):
        rows = [codes_of[s][x3][tile] for x3 in range(X3) for tile in range(2)]
        rows = jnp.concatenate(rows + rows[:2], axis=0)
        out_ref[flip(s, 4), 2 * Q * 32 : B_ROWS, :] = rows.astype(jnp.int32).astype(jnp.int16)


def line_kernel(got_ref, w_ref, out_ref, x_ref):
    first = pl.program_id(0) * T_BLOCK
    low_half = lax.broadcasted_iota(jnp.int32, (1, KW), 1) < 64
    for t in range(T_BLOCK):
        triple = flip(first + t, 3)
        scale = [
            scales_of(from_codes(got_ref[triple, p, 2 * Q * 32 : B_ROWS, :])) for p in range(2)
        ]
        for x3 in range(X3):
            row = (t * X3 + x3) * 32
            for tile in range(2):
                n = x3 * 2 + tile
                for c in range(2):
                    base = n * 64 + c * 32
                    v0, v1 = (
                        decode(got_ref, (triple, p), base, 32, scale[p][n : n + 1])
                        for p in range(2)
                    )
                    for half in range(2):
                        value = jnp.where(low_half, v0, v1) if half == 0 else jnp.where(low_half, v1, v0)
                        high, low = halves(value)
                        rho = 2 * tile + half
                        for third, part in enumerate((high, low)):
                            x_ref[rho, third * 2 + c, row : row + 32, :] = part
    parts = []
    for rho in range(4):
        table = w_ref[rho]
        lines = jnp.concatenate([x_ref[rho, n] for n in (0, 1, 2, 3, 0, 1)], axis=1)
        parts.append(dot(lines, jnp.concatenate([table[:256], table], axis=0)))
    for row in range(T_BLOCK * X3):
        at = slice(row * 32, (row + 1) * 32)
        out = radix_4([p[at, :KW] for p in parts], [p[at, KW:] for p in parts])
        for a in range(4):
            for c in range(2):
                out_ref[c, row, :, a * KW : (a + 1) * KW] = out[a][c]


def per_device(samples, kernels, dest, plane_off, kernel_id):
    z_table, y_table = constants()
    params = pltpu.CompilerParams(
        dimension_semantics=("arbitrary",), vmem_limit_bytes=VMEM_LIMIT
    )
    whole = pl.BlockSpec(memory_space=pltpu.VMEM)
    sources = [dest.reshape(ITEMS), plane_off, kernel_id, samples, kernels]
    packed = pl.pallas_call(
        spread_kernel,
        name="spread",
        out_shape=jax.ShapeDtypeStruct((N_DEST, A_ROWS, KW), jnp.int16),
        in_specs=[pl.BlockSpec(memory_space=pltpu.HBM)] * 5,
        out_specs=whole,
        scratch_shapes=[
            pltpu.SMEM((ITEMS,), jnp.int32),
            pltpu.SMEM((ITEMS,), jnp.int32),
            pltpu.SMEM((ITEMS,), jnp.int32),
            pltpu.VMEM((ITEMS, 2, XW, KW), jnp.bfloat16),
            pltpu.VMEM((ITEMS, KW, KW), jnp.bfloat16),
            pltpu.VMEM((2, STEP_ITEMS, KW, KW), jnp.bfloat16),
            pltpu.VMEM((2 * ROWS * PITCH, KW), jnp.float32),
            pltpu.VMEM((16, KW), jnp.int32),
            pltpu.SemaphoreType.DMA((3,)),
            pltpu.SemaphoreType.DMA((ITEMS // STEP_ITEMS,)),
            pltpu.SemaphoreType.DMA((ITEMS // STEP_ITEMS,)),
        ],
        compiler_params=pltpu.CompilerParams(vmem_limit_bytes=VMEM_LIMIT),
    )(*[pltpu.with_memory_space_constraint(source, pltpu.HBM) for source in sources])
    got = lax.all_to_all(packed, ("img", "slab"), split_axis=0, concat_axis=0, tiled=True)
    planes = pl.pallas_call(
        plane_kernel,
        name="plane",
        out_shape=jax.ShapeDtypeStruct((N_SLAB, B_ROWS, KW), jnp.int16),
        in_specs=[whole, whole],
        out_specs=whole,
        scratch_shapes=[
            pltpu.VMEM((2, 8, NZ, KW), jnp.bfloat16),
            pltpu.VMEM((X3, 2, 2, 2048, KW), jnp.bfloat16),
            pltpu.VMEM((X3, 4, 256, 256), jnp.float32),
            pltpu.VMEM((N_DEST, 8, KW), jnp.float32),
        ],
        compiler_params=pltpu.CompilerParams(vmem_limit_bytes=VMEM_LIMIT),
    )(got, jnp.asarray(z_table))
    lines = lax.all_to_all(
        planes,
        "slab",
        split_axis=0,
        concat_axis=0,
        tiled=True,
        axis_index_groups=[[flip(s, 4) for s in range(N_SLAB)]],
    )
    lines = lines.reshape(N_SLAB // 2, 2, B_ROWS, KW)
    rows = T_BLOCK * X3
    return pl.pallas_call(
        line_kernel,
        name="line",
        out_shape=jax.ShapeDtypeStruct((2, X_OWN, NZ // N_SLAB, NY), jnp.float32),
        grid=(8 // T_BLOCK,),
        in_specs=[
            whole,
            whole,
        ],
        out_specs=pl.BlockSpec((2, rows, NZ // N_SLAB, NY), lambda i: (0, i, 0, 0)),
        scratch_shapes=[pltpu.VMEM((4, 4, rows * 32, KW), jnp.bfloat16)],
        compiler_params=params,
    )(lines, jnp.asarray(y_table))


def solution(mesh):
    in_specs = (
        P(("half", "slab", "img"), None, None, None),
        P(),
        P(("half", "slab", "img"), None),
        P(("half", "slab", "img")),
        P(("half", "slab", "img")),
    )
    out_specs = P(None, ("half", "img"), "slab", None)
    return jax.shard_map(
        per_device, mesh=mesh, in_specs=in_specs, out_specs=out_specs, check_vma=False
    )
```

```python
import functools
import math

import jax
import jax.numpy as jnp
import ml_dtypes
import numpy as np
from jax import lax
from jax.experimental import pallas as pl
from jax.experimental.pallas import tpu as pltpu
from jax.sharding import PartitionSpec as P

NY = 512
NZ = 512
KW = 128
N_SLAB = 16
N_IMG = 4
N_DEST = N_SLAB * N_IMG
ITEMS = 64
XW = 96
X_OWN = XW // N_IMG
X3 = 3
ROWS = 2 * XW
Q = 2 * X3
A_ROWS = Q * 32 + 8
B_ROWS = 2 * Q * 32 + 8
PITCH = 33
LEVEL = 32700.0
TINY = 1e-30
STEP_ITEMS = 16
UNROLL = 16
T_BLOCK = 2
VMEM_LIMIT = 28 * 1024 * 1024


def swap_pairs(slab):
    return ((slab & 5) << 1) | ((slab >> 1) & 5)


def split_bf16(values):
    high = values.astype(ml_dtypes.bfloat16)
    low = (values - high.astype(np.float64)).astype(ml_dtypes.bfloat16)
    return high, low


def y_orders():
    lane = np.arange(KW)
    order = {}
    for pair in range(2):
        a, b, c, d = (0, 1, 2, 3) if pair == 0 else (1, 0, 3, 2)
        for b1, runs in enumerate(((a, c, b, d), (c, a, d, b))):
            order[pair, b1] = np.concatenate([4 * np.arange(32) + r for r in runs])
    y = {key: (2 * key[0] + key[1]) * KW + j for key, j in order.items()}
    near = (lane & 32) == 0
    first = [np.where(near, y[p, 0], y[p, 1]) for p in range(2)]
    second = [np.where(near, y[p, 1], y[p, 0]) for p in range(2)]
    low = lane < 64
    tiles = [
        np.where(low, first[0], first[1]),
        np.where(low, first[1], first[0]),
        np.where(low, second[0], second[1]),
        np.where(low, second[1], second[0]),
    ]
    for rho in range(4):
        assert np.all(tiles[rho] % 4 == rho)
    return tiles


@functools.lru_cache(None)
def constants():
    tiles = y_orders()
    k = np.arange(128)
    z_tables, y_tables = [], []
    for rho in range(4):
        factor = np.exp(2j * np.pi * (np.outer(k, 4 * k + rho) % NZ) / NZ)
        high, low = split_bf16(
            np.block([[factor.real, -factor.imag], [factor.imag, factor.real]])
        )
        z_tables.append(np.stack([t[:, n : n + KW] for t in (high, low) for n in (0, KW)]))
        factor = np.exp(2j * np.pi * (np.outer(tiles[rho], k) % NY) / NY) / math.sqrt(NY * NZ)
        high, low = split_bf16(
            np.block([[factor.real, factor.imag], [-factor.imag, factor.real]])
        )
        y_tables.append(np.concatenate([high, low], axis=0))
    return np.stack(z_tables), np.stack(y_tables)


def dot(a, b):
    return jnp.dot(a, b, preferred_element_type=jnp.float32)


def halves(value):
    high = value.astype(jnp.bfloat16)
    return high, (value - high.astype(jnp.float32)).astype(jnp.bfloat16)


def scale_codes(largest):
    return jnp.ceil(jnp.log2(jnp.maximum(largest, TINY)) * 256.0)


def to_codes(value, inverse):
    return jnp.round(value * inverse).astype(jnp.int32).astype(jnp.int16)


def from_codes(codes):
    return codes.astype(jnp.int32).astype(jnp.float32)


def decode(ref, lead, base, rows, scale):
    parts = [
        from_codes(ref[(*lead, slice(at, at + 8), slice(None))]) * scale
        for at in range(base, base + rows, 8)
    ]
    return jnp.concatenate(parts, axis=0)


def scales_of(tail):
    return jnp.exp2(tail * (1.0 / 256.0)) * (1.0 / LEVEL)


def radix_4(re, im):
    sr, dr, tr, er = re[0] + re[2], re[0] - re[2], re[1] + re[3], re[1] - re[3]
    si, di, ti, ei = im[0] + im[2], im[0] - im[2], im[1] + im[3], im[1] - im[3]
    return (sr + tr, si + ti), (dr - ei, di + er), (sr - tr, si - ti), (dr + ei, di - er)


def spread_kernel(
    dest_hbm, plane_hbm, kid_hbm, samples_hbm, kernels_hbm, out_ref,
    dest_s, plane_s, kid_s, samples_ref, kernels_ref, table_ref, rows_ref, label_ref,
    index_sem, samples_sem, kernels_sem,
):
    lane = lax.broadcasted_iota(jnp.int32, (1, KW), 1)
    sub = lax.broadcasted_iota(jnp.int32, (8, KW), 0)

    def samples_copy(step):
        at = pl.ds(step * STEP_ITEMS, STEP_ITEMS)
        return pltpu.make_async_copy(samples_hbm.at[at], samples_ref.at[at], samples_sem.at[step])

    def kernel_copy(step, item):
        return pltpu.make_async_copy(
            kernels_hbm.at[kid_s[item]], kernels_ref.at[item], kernels_sem.at[step]
        )

    def kernels_wait(step):
        at = pl.ds(step * STEP_ITEMS, STEP_ITEMS)
        pltpu.make_async_copy(
            kernels_hbm.at[pl.ds(0, STEP_ITEMS)], kernels_ref.at[at], kernels_sem.at[step]
        ).wait()

    index_copies = [
        pltpu.make_async_copy(src, dst, index_sem.at[n])
        for n, (src, dst) in enumerate(
            ((kid_hbm, kid_s), (dest_hbm, dest_s), (plane_hbm, plane_s))
        )
    ]
    for copy in index_copies:
        copy.start()
    samples_copy(0).start()
    label_ref[...] = jnp.zeros_like(label_ref)
    run, within = lane >> 5, lane & 31
    orders = [
        jnp.broadcast_to(4 * within + 2 * ((run & 1) ^ b1) + ((run >> 1) ^ pair), (KW, KW))
        for pair in range(2)
        for b1 in range(2)
    ]
    index_copies[0].wait()
    for step in range(ITEMS // STEP_ITEMS):
        if step > 0:
            samples_copy(step).start()
        for u in range(STEP_ITEMS):
            kernel_copy(step, step * STEP_ITEMS + u).start()
    for copy in index_copies[1:]:
        copy.wait()

    def order_columns(step):
        for u in range(STEP_ITEMS):
            table = kernels_ref[step * STEP_ITEMS + u].astype(jnp.float32)
            table = jnp.take_along_axis(table, orders[u % 4], axis=1, mode="promise_in_bounds")
            table_ref[step % 2, u] = table.astype(jnp.bfloat16)

    kernels_wait(0)
    order_columns(0)
    steps = ITEMS // STEP_ITEMS
    for step in range(steps):
        samples_copy(step).wait()
        if step + 1 < steps:
            kernels_wait(step + 1)
        for u in range(STEP_ITEMS):
            item = step * STEP_ITEMS + u
            pair, b1 = u % 4 // 2, u % 2
            g = item // 4
            value = dot(samples_ref[item].reshape(ROWS, KW), table_ref[step % 2, u])
            rows_ref[pl.ds(pair * ROWS * PITCH + b1 * 16 + g, ROWS, stride=PITCH), :] = value
            d = dest_s[item]
            flipped = ((d & 1) << 3) | ((d & 2) << 1) | ((d & 4) >> 1) | ((d & 8) >> 3)
            plane = plane_s[item] * 16 + flipped
            place = (plane & 3) * 128 + (plane >> 2)
            row = 8 * pair + 6 + b1
            label_ref[row : row + 1, :] = jnp.where(
                (lane & 15) == g, place, label_ref[row : row + 1, :]
            )
        if step + 1 < steps:
            order_columns(step + 1)

    def encode(d, carry):
        slab = swap_pairs(d & (N_SLAB - 1))
        pair = slab >> 3
        first = pair * ROWS + X_OWN * (d >> 4) + X3 * (slab & 7)
        values, tops = [], []
        for r in range(2):
            for x3 in range(X3):
                value = rows_ref[pl.ds((first + r * XW + x3) * PITCH, 32), :]
                values.append(value)
                tops.append(jnp.max(jnp.abs(value), axis=0, keepdims=True))
        codes = scale_codes(jnp.concatenate(tops + [tops[0], tops[0]], axis=0))
        inverse = jnp.exp2(codes * (-1.0 / 256.0)) * LEVEL
        for q in range(Q):
            out_ref[d, q * 32 : (q + 1) * 32, :] = to_codes(values[q], inverse[q : q + 1])
        labels = label_ref[pl.ds(pl.multiple_of(pair * 8, 8), 8), :]
        tail = jnp.where(sub < Q, codes.astype(jnp.int32), labels)
        out_ref[d, Q * 32 : A_ROWS, :] = tail.astype(jnp.int16)
        return carry

    lax.fori_loop(0, N_DEST, encode, 0, unroll=UNROLL)


def plane_kernel(got_ref, w_ref, out_ref, hot_ref, x_ref, freq_ref, scale_ref):
    lane = lax.broadcasted_iota(jnp.int32, (1, KW), 1)
    place = lax.broadcasted_iota(jnp.int32, (NZ, KW), 0).astype(jnp.int16)
    one, zero = jnp.ones((), jnp.bfloat16), jnp.zeros((), jnp.bfloat16)
    near = (lane & 32) == 0
    for group in range(8):
        rows = [jnp.zeros((1, KW), jnp.int32), jnp.zeros((1, KW), jnp.int32)]
        for e in range(8):
            src = group * 8 + e
            tail = got_ref[src, Q * 32 : A_ROWS, :].astype(jnp.int32)
            scale_ref[src] = scales_of(tail.astype(jnp.float32))
            for b1 in range(2):
                rows[b1] = jnp.where((lane >> 4) == e, tail[6 + b1 : 7 + b1], rows[b1])
        for b1 in range(2):
            hit = jnp.where(place == rows[b1].astype(jnp.int16), one, zero)
            hot_ref[b1, group] = hit
    codes_of = [[[None] * 2 for _ in range(X3)] for _ in range(N_SLAB)]
    for x3 in range(X3):
        for src in range(N_DEST):
            for r in range(2):
                q = r * X3 + x3
                for b1 in range(2):
                    base = q * 32 + b1 * 16
                    value = decode(got_ref, (src,), base, 16, scale_ref[src, q : q + 1, :])
                    high, low = halves(value)
                    x_ref[x3, b1, r, src * 16 : src * 16 + 16, :] = high
                    x_ref[x3, b1, r, 1024 + src * 16 : 1040 + src * 16, :] = low
        grid = [
            dot(
                jnp.concatenate([hot_ref[b1, group] for group in range(8)] * 2, axis=1),
                jnp.concatenate([x_ref[x3, b1, r] for r in range(2)], axis=1),
            )
            for b1 in range(2)
        ]
        for rho in range(4):
            at = slice(rho * 128, (rho + 1) * 128)
            parts = []
            for r in range(2):
                cols = slice(r * KW, (r + 1) * KW)
                t0, t1 = grid[0][at, cols], grid[1][at, cols]
                parts.append(
                    jnp.concatenate([jnp.where(near, t0, t1), jnp.where(near, t1, t0)], axis=1)
                )
            high, low = halves(jnp.concatenate(parts, axis=0))
            table = [jnp.concatenate([w_ref[rho, n], w_ref[rho, n + 1]], axis=1) for n in (0, 2)]
            both = dot(jnp.concatenate(table, axis=0), high)
            freq_ref[x3, rho] = both[:256] + both[256:] + dot(table[0], low)
        for kk in range(4):
            tops = [[], [], [], []]
            for tile in range(2):
                cols = slice(tile * KW, (tile + 1) * KW)
                at_re, at_im = slice(kk * 32, kk * 32 + 32), slice(128 + kk * 32, 160 + kk * 32)
                out = radix_4(
                    [freq_ref[x3, rho, at_re, cols] for rho in range(4)],
                    [freq_ref[x3, rho, at_im, cols] for rho in range(4)],
                )
                for a in range(4):
                    freq_ref[x3, a, at_re, cols] = out[a][0]
                    freq_ref[x3, a, at_im, cols] = out[a][1]
                    top = jnp.maximum(jnp.abs(out[a][0]), jnp.abs(out[a][1]))
                    tops[a].append(jnp.max(top, axis=0, keepdims=True))
            codes = scale_codes(jnp.concatenate(tops[0] + tops[1] + tops[2] + tops[3], axis=0))
            inverse = jnp.exp2(codes * (-1.0 / 256.0)) * LEVEL
            for a in range(4):
                for tile in range(2):
                    cols = slice(tile * KW, (tile + 1) * KW)
                    n = 2 * a + tile
                    codes_of[4 * a + kk][x3][tile] = codes[n : n + 1]
                    base = (x3 * 2 + tile) * 64
                    for c in range(2):
                        value = freq_ref[x3, a, c * 128 + kk * 32 : c * 128 + kk * 32 + 32, cols]
                        out_ref[4 * a + kk, base + c * 32 : base + c * 32 + 32, :] = to_codes(
                            value, inverse[n : n + 1]
                        )
    for s in range(N_SLAB):
        rows = [codes_of[s][x3][tile] for x3 in range(X3) for tile in range(2)]
        rows = jnp.concatenate(rows + rows[:2], axis=0)
        out_ref[s, 2 * Q * 32 : B_ROWS, :] = rows.astype(jnp.int32).astype(jnp.int16)


def line_kernel(got_ref, w_ref, out_ref, x_ref):
    first = pl.program_id(0) * T_BLOCK
    low_half = lax.broadcasted_iota(jnp.int32, (1, KW), 1) < 64
    for t in range(T_BLOCK):
        scale = [
            scales_of(from_codes(got_ref[p, first + t, 2 * Q * 32 : B_ROWS, :])) for p in range(2)
        ]
        for x3 in range(X3):
            row = (t * X3 + x3) * 32
            for tile in range(2):
                n = x3 * 2 + tile
                for c in range(2):
                    base = n * 64 + c * 32
                    v0, v1 = (
                        decode(got_ref, (p, first + t), base, 32, scale[p][n : n + 1])
                        for p in range(2)
                    )
                    for half in range(2):
                        value = jnp.where(low_half, v0, v1) if half == 0 else jnp.where(low_half, v1, v0)
                        high, low = halves(value)
                        rho = 2 * tile + half
                        for third, part in enumerate((high, low)):
                            x_ref[rho, third * 2 + c, row : row + 32, :] = part
    parts = []
    for rho in range(4):
        table = w_ref[rho]
        lines = jnp.concatenate([x_ref[rho, n] for n in (0, 1, 2, 3, 0, 1)], axis=1)
        parts.append(dot(lines, jnp.concatenate([table[:256], table], axis=0)))
    for row in range(T_BLOCK * X3):
        at = slice(row * 32, (row + 1) * 32)
        out = radix_4([p[at, :KW] for p in parts], [p[at, KW:] for p in parts])
        for a in range(4):
            for c in range(2):
                out_ref[c, row, :, a * KW : (a + 1) * KW] = out[a][c]


def per_device(samples, kernels, dest, plane_off, kernel_id):
    z_table, y_table = constants()
    params = pltpu.CompilerParams(
        dimension_semantics=("arbitrary",), vmem_limit_bytes=VMEM_LIMIT
    )
    whole = pl.BlockSpec(memory_space=pltpu.VMEM)
    sources = [dest.reshape(ITEMS), plane_off, kernel_id, samples, kernels]
    packed = pl.pallas_call(
        spread_kernel,
        name="spread",
        out_shape=jax.ShapeDtypeStruct((N_DEST, A_ROWS, KW), jnp.int16),
        in_specs=[pl.BlockSpec(memory_space=pltpu.HBM)] * 5,
        out_specs=whole,
        scratch_shapes=[
            pltpu.SMEM((ITEMS,), jnp.int32),
            pltpu.SMEM((ITEMS,), jnp.int32),
            pltpu.SMEM((ITEMS,), jnp.int32),
            pltpu.VMEM((ITEMS, 2, XW, KW), jnp.bfloat16),
            pltpu.VMEM((ITEMS, KW, KW), jnp.bfloat16),
            pltpu.VMEM((2, STEP_ITEMS, KW, KW), jnp.bfloat16),
            pltpu.VMEM((2 * ROWS * PITCH, KW), jnp.float32),
            pltpu.VMEM((16, KW), jnp.int32),
            pltpu.SemaphoreType.DMA((3,)),
            pltpu.SemaphoreType.DMA((ITEMS // STEP_ITEMS,)),
            pltpu.SemaphoreType.DMA((ITEMS // STEP_ITEMS,)),
        ],
        compiler_params=pltpu.CompilerParams(vmem_limit_bytes=VMEM_LIMIT),
    )(*[pltpu.with_memory_space_constraint(source, pltpu.HBM) for source in sources])
    order = [swap_pairs(s) * N_IMG + m for m in range(N_IMG) for s in range(N_SLAB)]
    got = lax.all_to_all(
        packed,
        ("slab", "img"),
        split_axis=0,
        concat_axis=0,
        tiled=True,
        axis_index_groups=[order],
    )
    planes = pl.pallas_call(
        plane_kernel,
        name="plane",
        out_shape=jax.ShapeDtypeStruct((N_SLAB, B_ROWS, KW), jnp.int16),
        in_specs=[whole, whole],
        out_specs=whole,
        scratch_shapes=[
            pltpu.VMEM((2, 8, NZ, KW), jnp.bfloat16),
            pltpu.VMEM((X3, 2, 2, 2048, KW), jnp.bfloat16),
            pltpu.VMEM((X3, 4, 256, 256), jnp.float32),
            pltpu.VMEM((N_DEST, 8, KW), jnp.float32),
        ],
        compiler_params=pltpu.CompilerParams(vmem_limit_bytes=VMEM_LIMIT),
    )(got, jnp.asarray(z_table))
    lines = lax.all_to_all(planes, "slab", split_axis=0, concat_axis=0, tiled=True)
    lines = lines.reshape(2, N_SLAB // 2, B_ROWS, KW)
    rows = T_BLOCK * X3
    return pl.pallas_call(
        line_kernel,
        name="line",
        out_shape=jax.ShapeDtypeStruct((2, X_OWN, NZ // N_SLAB, NY), jnp.float32),
        grid=(8 // T_BLOCK,),
        in_specs=[
            whole,
            whole,
        ],
        out_specs=pl.BlockSpec((2, rows, NZ // N_SLAB, NY), lambda i: (0, i, 0, 0)),
        scratch_shapes=[pltpu.VMEM((4, 4, rows * 32, KW), jnp.bfloat16)],
        compiler_params=params,
    )(lines, jnp.asarray(y_table))


def solution(mesh):
    in_specs = (
        P(("half", "slab", "img"), None, None, None),
        P(),
        P(("half", "slab", "img"), None),
        P(("half", "slab", "img")),
        P(("half", "slab", "img")),
    )
    out_specs = P(None, ("half", "img"), "slab", None)
    return jax.shard_map(
        per_device, mesh=mesh, in_specs=in_specs, out_specs=out_specs, check_vma=False
    )
```

```python
import functools
import math

import jax
import jax.numpy as jnp
import ml_dtypes
import numpy as np
from jax import lax
from jax.experimental import pallas as pl
from jax.experimental.pallas import tpu as pltpu
from jax.sharding import PartitionSpec as P

NY = 512
NZ = 512
KW = 128
N_SLAB = 16
N_IMG = 4
N_DEST = N_SLAB * N_IMG
ITEMS = 64
XW = 96
X_OWN = XW // N_IMG
X3 = 3
ROWS = 2 * XW
Q = 2 * X3
A_ROWS = Q * 32 + 8
B_ROWS = 2 * Q * 32 + 8
PITCH = 33
LEVEL = 32700.0
TINY = 1e-30
STEP_ITEMS = 16
UNROLL = 16
T_BLOCK = 4
VMEM_LIMIT = 28 * 1024 * 1024


def split_bf16(values):
    high = values.astype(ml_dtypes.bfloat16)
    low = (values - high.astype(np.float64)).astype(ml_dtypes.bfloat16)
    return high, low


def y_orders():
    lane = np.arange(KW)
    order = {}
    for pair in range(2):
        a, b, c, d = (0, 1, 2, 3) if pair == 0 else (1, 0, 3, 2)
        for b1, runs in enumerate(((a, c, b, d), (c, a, d, b))):
            order[pair, b1] = np.concatenate([4 * np.arange(32) + r for r in runs])
    y = {key: (2 * key[0] + key[1]) * KW + j for key, j in order.items()}
    near = (lane & 32) == 0
    first = [np.where(near, y[p, 0], y[p, 1]) for p in range(2)]
    second = [np.where(near, y[p, 1], y[p, 0]) for p in range(2)]
    low = lane < 64
    tiles = [
        np.where(low, first[0], first[1]),
        np.where(low, first[1], first[0]),
        np.where(low, second[0], second[1]),
        np.where(low, second[1], second[0]),
    ]
    for rho in range(4):
        assert np.all(tiles[rho] % 4 == rho)
    return tiles


@functools.lru_cache(None)
def constants():
    tiles = y_orders()
    k = np.arange(128)
    z_tables, y_tables = [], []
    for rho in range(4):
        factor = np.exp(2j * np.pi * (np.outer(k, 4 * k + rho) % NZ) / NZ)
        high, low = split_bf16(
            np.block([[factor.real, -factor.imag], [factor.imag, factor.real]])
        )
        z_tables.append(np.stack([t[:, n : n + KW] for t in (high, low) for n in (0, KW)]))
        factor = np.exp(2j * np.pi * (np.outer(tiles[rho], k) % NY) / NY) / math.sqrt(NY * NZ)
        high, low = split_bf16(
            np.block([[factor.real, factor.imag], [-factor.imag, factor.real]])
        )
        y_tables.append(np.concatenate([high, low], axis=0))
    return np.stack(z_tables), np.stack(y_tables)


def dot(a, b):
    return jnp.dot(a, b, preferred_element_type=jnp.float32)


def halves(value):
    high = value.astype(jnp.bfloat16)
    return high, (value - high.astype(jnp.float32)).astype(jnp.bfloat16)


def scale_codes(largest):
    return jnp.ceil(jnp.log2(jnp.maximum(largest, TINY)) * 256.0)


def to_codes(value, inverse):
    return jnp.round(value * inverse).astype(jnp.int32).astype(jnp.int16)


def from_codes(codes):
    return codes.astype(jnp.int32).astype(jnp.float32)


def decode(ref, lead, base, rows, scale):
    parts = [
        from_codes(ref[(*lead, slice(at, at + 8), slice(None))]) * scale
        for at in range(base, base + rows, 8)
    ]
    return jnp.concatenate(parts, axis=0)


def scales_of(tail):
    return jnp.exp2(tail * (1.0 / 256.0)) * (1.0 / LEVEL)


def radix_4(re, im):
    sr, dr, tr, er = re[0] + re[2], re[0] - re[2], re[1] + re[3], re[1] - re[3]
    si, di, ti, ei = im[0] + im[2], im[0] - im[2], im[1] + im[3], im[1] - im[3]
    return (sr + tr, si + ti), (dr - ei, di + er), (sr - tr, si - ti), (dr + ei, di - er)


def spread_kernel(
    dest_hbm, plane_hbm, kid_hbm, samples_hbm, kernels_hbm, out_ref,
    dest_s, plane_s, kid_s, samples_ref, kernels_ref, table_ref, rows_ref, label_ref,
    index_sem, samples_sem, kernels_sem,
):
    lane = lax.broadcasted_iota(jnp.int32, (1, KW), 1)
    sub = lax.broadcasted_iota(jnp.int32, (8, KW), 0)

    def samples_copy(step):
        at = pl.ds(step * STEP_ITEMS, STEP_ITEMS)
        return pltpu.make_async_copy(samples_hbm.at[at], samples_ref.at[at], samples_sem.at[step])

    def kernel_copy(step, item):
        return pltpu.make_async_copy(
            kernels_hbm.at[kid_s[item]], kernels_ref.at[item], kernels_sem.at[step]
        )

    def kernels_wait(step):
        at = pl.ds(step * STEP_ITEMS, STEP_ITEMS)
        pltpu.make_async_copy(
            kernels_hbm.at[pl.ds(0, STEP_ITEMS)], kernels_ref.at[at], kernels_sem.at[step]
        ).wait()

    index_copies = [
        pltpu.make_async_copy(src, dst, index_sem.at[n])
        for n, (src, dst) in enumerate(
            ((kid_hbm, kid_s), (dest_hbm, dest_s), (plane_hbm, plane_s))
        )
    ]
    for copy in index_copies:
        copy.start()
    samples_copy(0).start()
    label_ref[...] = jnp.zeros_like(label_ref)
    run, within = lane >> 5, lane & 31
    orders = [
        jnp.broadcast_to(4 * within + 2 * ((run & 1) ^ b1) + ((run >> 1) ^ pair), (KW, KW))
        for pair in range(2)
        for b1 in range(2)
    ]
    index_copies[0].wait()
    for step in range(ITEMS // STEP_ITEMS):
        if step > 0:
            samples_copy(step).start()
        for u in range(STEP_ITEMS):
            kernel_copy(step, step * STEP_ITEMS + u).start()
    for copy in index_copies[1:]:
        copy.wait()

    def order_columns(step):
        for u in range(STEP_ITEMS):
            table = kernels_ref[step * STEP_ITEMS + u].astype(jnp.float32)
            table = jnp.take_along_axis(table, orders[u % 4], axis=1, mode="promise_in_bounds")
            table_ref[step % 2, u] = table.astype(jnp.bfloat16)

    kernels_wait(0)
    order_columns(0)
    steps = ITEMS // STEP_ITEMS
    for step in range(steps):
        samples_copy(step).wait()
        if step + 1 < steps:
            kernels_wait(step + 1)
        for u in range(STEP_ITEMS):
            item = step * STEP_ITEMS + u
            pair, b1 = u % 4 // 2, u % 2
            g = item // 4
            value = dot(samples_ref[item].reshape(ROWS, KW), table_ref[step % 2, u])
            rows_ref[pl.ds(pair * ROWS * PITCH + b1 * 16 + g, ROWS, stride=PITCH), :] = value
            d = dest_s[item]
            flipped = ((d & 1) << 3) | ((d & 2) << 1) | ((d & 4) >> 1) | ((d & 8) >> 3)
            plane = plane_s[item] * 16 + flipped
            place = (plane & 3) * 128 + (plane >> 2)
            row = 8 * pair + 6 + b1
            label_ref[row : row + 1, :] = jnp.where(
                (lane & 15) == g, place, label_ref[row : row + 1, :]
            )
        if step + 1 < steps:
            order_columns(step + 1)

    def encode(d, carry):
        pair = (d % N_SLAB) // 8
        first = pair * ROWS + X_OWN * (d // N_SLAB) + X3 * (d % 8)
        values, tops = [], []
        for r in range(2):
            for x3 in range(X3):
                value = rows_ref[pl.ds((first + r * XW + x3) * PITCH, 32), :]
                values.append(value)
                tops.append(jnp.max(jnp.abs(value), axis=0, keepdims=True))
        codes = scale_codes(jnp.concatenate(tops + [tops[0], tops[0]], axis=0))
        inverse = jnp.exp2(codes * (-1.0 / 256.0)) * LEVEL
        for q in range(Q):
            out_ref[d, q * 32 : (q + 1) * 32, :] = to_codes(values[q], inverse[q : q + 1])
        labels = label_ref[pl.ds(pl.multiple_of(pair * 8, 8), 8), :]
        tail = jnp.where(sub < Q, codes.astype(jnp.int32), labels)
        out_ref[d, Q * 32 : A_ROWS, :] = tail.astype(jnp.int16)
        return carry

    lax.fori_loop(0, N_DEST, encode, 0, unroll=UNROLL)


def plane_kernel(got_ref, w_ref, out_ref, hot_ref, x_ref, freq_ref, scale_ref):
    lane = lax.broadcasted_iota(jnp.int32, (1, KW), 1)
    place = lax.broadcasted_iota(jnp.int32, (NZ, KW), 0).astype(jnp.int16)
    one, zero = jnp.ones((), jnp.bfloat16), jnp.zeros((), jnp.bfloat16)
    near = (lane & 32) == 0
    for group in range(8):
        rows = [jnp.zeros((1, KW), jnp.int32), jnp.zeros((1, KW), jnp.int32)]
        for e in range(8):
            src = group * 8 + e
            tail = got_ref[src, Q * 32 : A_ROWS, :].astype(jnp.int32)
            scale_ref[src] = scales_of(tail.astype(jnp.float32))
            for b1 in range(2):
                rows[b1] = jnp.where((lane >> 4) == e, tail[6 + b1 : 7 + b1], rows[b1])
        for b1 in range(2):
            hit = jnp.where(place == rows[b1].astype(jnp.int16), one, zero)
            hot_ref[b1, group] = hit
    codes_of = [[[None] * 2 for _ in range(X3)] for _ in range(N_SLAB)]
    for x3 in range(X3):
        for src in range(N_DEST):
            for r in range(2):
                q = r * X3 + x3
                for b1 in range(2):
                    base = q * 32 + b1 * 16
                    value = decode(got_ref, (src,), base, 16, scale_ref[src, q : q + 1, :])
                    high, low = halves(value)
                    x_ref[x3, b1, r, src * 16 : src * 16 + 16, :] = high
                    x_ref[x3, b1, r, 1024 + src * 16 : 1040 + src * 16, :] = low
        grid = [
            dot(
                jnp.concatenate([hot_ref[b1, group] for group in range(8)] * 2, axis=1),
                jnp.concatenate([x_ref[x3, b1, r] for r in range(2)], axis=1),
            )
            for b1 in range(2)
        ]
        for rho in range(4):
            at = slice(rho * 128, (rho + 1) * 128)
            parts = []
            for r in range(2):
                cols = slice(r * KW, (r + 1) * KW)
                t0, t1 = grid[0][at, cols], grid[1][at, cols]
                parts.append(
                    jnp.concatenate([jnp.where(near, t0, t1), jnp.where(near, t1, t0)], axis=1)
                )
            high, low = halves(jnp.concatenate(parts, axis=0))
            table = jnp.concatenate([w_ref[rho, n] for n in (0, 1, 0, 1, 2, 3)], axis=1)
            freq_ref[x3, rho] = dot(table, jnp.concatenate([high, low, high], axis=0))
        for kk in range(4):
            tops = [[], [], [], []]
            for tile in range(2):
                cols = slice(tile * KW, (tile + 1) * KW)
                at_re, at_im = slice(kk * 32, kk * 32 + 32), slice(128 + kk * 32, 160 + kk * 32)
                out = radix_4(
                    [freq_ref[x3, rho, at_re, cols] for rho in range(4)],
                    [freq_ref[x3, rho, at_im, cols] for rho in range(4)],
                )
                for a in range(4):
                    freq_ref[x3, a, at_re, cols] = out[a][0]
                    freq_ref[x3, a, at_im, cols] = out[a][1]
                    top = jnp.maximum(jnp.abs(out[a][0]), jnp.abs(out[a][1]))
                    tops[a].append(jnp.max(top, axis=0, keepdims=True))
            codes = scale_codes(jnp.concatenate(tops[0] + tops[1] + tops[2] + tops[3], axis=0))
            inverse = jnp.exp2(codes * (-1.0 / 256.0)) * LEVEL
            for a in range(4):
                for tile in range(2):
                    cols = slice(tile * KW, (tile + 1) * KW)
                    n = 2 * a + tile
                    codes_of[4 * a + kk][x3][tile] = codes[n : n + 1]
                    base = (x3 * 2 + tile) * 64
                    for c in range(2):
                        value = freq_ref[x3, a, c * 128 + kk * 32 : c * 128 + kk * 32 + 32, cols]
                        out_ref[4 * a + kk, base + c * 32 : base + c * 32 + 32, :] = to_codes(
                            value, inverse[n : n + 1]
                        )
    for s in range(N_SLAB):
        rows = [codes_of[s][x3][tile] for x3 in range(X3) for tile in range(2)]
        rows = jnp.concatenate(rows + rows[:2], axis=0)
        out_ref[s, 2 * Q * 32 : B_ROWS, :] = rows.astype(jnp.int32).astype(jnp.int16)


def line_kernel(got_ref, w_ref, out_ref, x_ref):
    first = pl.program_id(0) * T_BLOCK
    low_half = lax.broadcasted_iota(jnp.int32, (1, KW), 1) < 64
    for t in range(T_BLOCK):
        scale = [
            scales_of(from_codes(got_ref[p, first + t, 2 * Q * 32 : B_ROWS, :])) for p in range(2)
        ]
        for x3 in range(X3):
            row = (t * X3 + x3) * 32
            for tile in range(2):
                n = x3 * 2 + tile
                for c in range(2):
                    base = n * 64 + c * 32
                    v0, v1 = (
                        decode(got_ref, (p, first + t), base, 32, scale[p][n : n + 1])
                        for p in range(2)
                    )
                    for half in range(2):
                        value = jnp.where(low_half, v0, v1) if half == 0 else jnp.where(low_half, v1, v0)
                        high, low = halves(value)
                        rho = 2 * tile + half
                        for third, part in enumerate((high, low)):
                            x_ref[rho, third * 2 + c, row : row + 32, :] = part
    parts = []
    for rho in range(4):
        table = w_ref[rho]
        lines = jnp.concatenate([x_ref[rho, n] for n in (0, 1, 2, 3, 0, 1)], axis=1)
        parts.append(dot(lines, jnp.concatenate([table[:256], table], axis=0)))
    for row in range(T_BLOCK * X3):
        at = slice(row * 32, (row + 1) * 32)
        out = radix_4([p[at, :KW] for p in parts], [p[at, KW:] for p in parts])
        for a in range(4):
            for c in range(2):
                out_ref[c, row, :, a * KW : (a + 1) * KW] = out[a][c]


def per_device(samples, kernels, dest, plane_off, kernel_id):
    z_table, y_table = constants()
    params = pltpu.CompilerParams(
        dimension_semantics=("arbitrary",), vmem_limit_bytes=VMEM_LIMIT
    )
    whole = pl.BlockSpec(memory_space=pltpu.VMEM)
    sources = [dest.reshape(ITEMS), plane_off, kernel_id, samples, kernels]
    packed = pl.pallas_call(
        spread_kernel,
        name="spread",
        out_shape=jax.ShapeDtypeStruct((N_DEST, A_ROWS, KW), jnp.int16),
        in_specs=[pl.BlockSpec(memory_space=pltpu.HBM)] * 5,
        out_specs=whole,
        scratch_shapes=[
            pltpu.SMEM((ITEMS,), jnp.int32),
            pltpu.SMEM((ITEMS,), jnp.int32),
            pltpu.SMEM((ITEMS,), jnp.int32),
            pltpu.VMEM((ITEMS, 2, XW, KW), jnp.bfloat16),
            pltpu.VMEM((ITEMS, KW, KW), jnp.bfloat16),
            pltpu.VMEM((2, STEP_ITEMS, KW, KW), jnp.bfloat16),
            pltpu.VMEM((2 * ROWS * PITCH, KW), jnp.float32),
            pltpu.VMEM((16, KW), jnp.int32),
            pltpu.SemaphoreType.DMA((3,)),
            pltpu.SemaphoreType.DMA((ITEMS // STEP_ITEMS,)),
            pltpu.SemaphoreType.DMA((ITEMS // STEP_ITEMS,)),
        ],
        compiler_params=pltpu.CompilerParams(vmem_limit_bytes=VMEM_LIMIT),
    )(*[pltpu.with_memory_space_constraint(source, pltpu.HBM) for source in sources])
    got = lax.all_to_all(packed, ("img", "slab"), split_axis=0, concat_axis=0, tiled=True)
    planes = pl.pallas_call(
        plane_kernel,
        name="plane",
        out_shape=jax.ShapeDtypeStruct((N_SLAB, B_ROWS, KW), jnp.int16),
        in_specs=[whole, whole],
        out_specs=whole,
        scratch_shapes=[
            pltpu.VMEM((2, 8, NZ, KW), jnp.bfloat16),
            pltpu.VMEM((X3, 2, 2, 2048, KW), jnp.bfloat16),
            pltpu.VMEM((X3, 4, 256, 256), jnp.float32),
            pltpu.VMEM((N_DEST, 8, KW), jnp.float32),
        ],
        compiler_params=pltpu.CompilerParams(vmem_limit_bytes=VMEM_LIMIT),
    )(got, jnp.asarray(z_table))
    lines = lax.all_to_all(planes, "slab", split_axis=0, concat_axis=0, tiled=True)
    lines = lines.reshape(2, N_SLAB // 2, B_ROWS, KW)
    rows = T_BLOCK * X3
    return pl.pallas_call(
        line_kernel,
        name="line",
        out_shape=jax.ShapeDtypeStruct((2, X_OWN, NZ // N_SLAB, NY), jnp.float32),
        grid=(8 // T_BLOCK,),
        in_specs=[
            whole,
            whole,
        ],
        out_specs=pl.BlockSpec((2, rows, NZ // N_SLAB, NY), lambda i: (0, i, 0, 0)),
        scratch_shapes=[pltpu.VMEM((4, 4, rows * 32, KW), jnp.bfloat16)],
        compiler_params=params,
    )(lines, jnp.asarray(y_table))


def solution(mesh):
    in_specs = (
        P(("half", "slab", "img"), None, None, None),
        P(),
        P(("half", "slab", "img"), None),
        P(("half", "slab", "img")),
        P(("half", "slab", "img")),
    )
    out_specs = P(None, ("half", "img"), "slab", None)
    return jax.shard_map(
        per_device, mesh=mesh, in_specs=in_specs, out_specs=out_specs, check_vma=False
    )
```
